32 devices in a mesh: req: 16 (over z, y, core), tp: 2 (over x).
Axes of the slice: x: 2, y: 2, z: 4, core: 2. Of those that a mesh axis runs over, the one named last changes fastest.
Arguments:
- queries: bfloat16 [96, 24, 8192], P('req', None, 'tp'), may hold values from -8 to 8
- fresh_kv: bfloat16 [96, 24, 2048], P('req', None, 'tp'), may hold values from -8 to 8
- key_value_pages: bfloat16 [832, 128, 2048], P('req', None, 'tp'), may hold values from -6 to 6
- cache_lengths: int32 [96], P('req'), may hold values from 1 to 4096, as said below
- page_table: int32 [96, 32], P('req'), may hold values from 0 to 51, as said below
- movers: int32 [16, 2], P('req'), may hold values from 0 to 5, as said below
- w_out: bfloat16 [4096, 8192], P('req', 'tp'), may hold values from -0.0625 to 0.0625
Outputs:
- projected: bfloat16 [2304, 4096], P('req', 'tp')
The draws below stay inside these ranges and needn't reach their ends.
Inputs may be any that keep to these rules, and one draw needn't show every extreme that they name: `cache_lengths`: in every draw one request holds exactly 4096 positions. `cache_lengths`: A request in a slot named by movers holds at most 512 positions, and in every draw one of them holds exactly that many. `page_table`: the entries that a request's length uses are distinct pages among all requests of its owner; the other entries are any pages of the pool. `movers`: the two slots of a row differ.
All inputs are finite; a program needn't handle non-finite values.
Results may differ from the reference program's by a relative error of at most 0.0057.
Values may be sent and summed in bfloat16 or wider, within the bound.
A program may use at most 320 MiB of HBM per device.

```python
import jax
import jax.numpy as jnp
from jax import lax

QUERY_HEADS = 64
KEY_VALUE_HEADS = 8
HEAD_SIZE = 128
DOUT = 4096
NEW_TOKENS = 24
PAGE_POSITIONS = 128
MAXP = 32
MIGP = 4
REQ_DEV = 6
OWNING_DEVICES = 16
TOTAL_REQUESTS = 96
PAGES_PER_DEVICE = 52
TOKENS = 2304


def layout(key):
    base_key = jax.random.fold_in(key, 11)
    keys_all = jax.random.split(base_key, 7)
    to_next = jax.random.randint(keys_all[0], (OWNING_DEVICES,), 0, REQ_DEV)
    to_prev = (to_next + 1 + jax.random.randint(keys_all[1], (OWNING_DEVICES,), 0, REQ_DEV - 1)) % REQ_DEV
    slot_ids = jnp.arange(REQ_DEV, dtype=jnp.int32)[None, :]
    device = jnp.arange(OWNING_DEVICES, dtype=jnp.int32)[:, None]
    moving = (slot_ids == to_next[:, None]) | (slot_ids == to_prev[:, None])
    exponent = jax.random.randint(keys_all[2], (OWNING_DEVICES, REQ_DEV), 0, 6)
    span = jnp.power(2, exponent)
    wanted = jax.random.randint(keys_all[3], (OWNING_DEVICES, REQ_DEV), 1, span + 1)
    long_owner = jax.random.randint(keys_all[4], (), 0, OWNING_DEVICES)
    short_owner = jax.random.randint(keys_all[5], (), 0, OWNING_DEVICES)
    first_stay = jnp.argmax(jnp.logical_not(moving).astype(jnp.int32), axis=1)
    long_slot = (device == long_owner) & (slot_ids == first_stay[:, None])
    short_slot = (device == short_owner) & (slot_ids == to_next[:, None])
    wanted = jnp.where(long_slot, MAXP, wanted)
    wanted = jnp.where(short_slot, MIGP, wanted)
    wanted = jnp.minimum(wanted, jnp.where(moving, MIGP, MAXP))
    ranking = slot_ids + REQ_DEV * jnp.logical_not(moving).astype(jnp.int32)
    ordering = jnp.argsort(ranking, axis=1)
    remaining = jnp.full((OWNING_DEVICES,), PAGES_PER_DEVICE, dtype=jnp.int32)
    page_list = jnp.zeros((OWNING_DEVICES, REQ_DEV), dtype=jnp.int32)
    owner_ids = jnp.arange(OWNING_DEVICES, dtype=jnp.int32)
    for position in range(REQ_DEV):
        chosen = ordering[:, position]
        want_here = jnp.take_along_axis(wanted, chosen[:, None], axis=1)[:, 0]
        granted = jnp.minimum(want_here, remaining - (REQ_DEV - 1 - position))
        page_list = page_list.at[owner_ids, chosen].set(granted)
        remaining = remaining - granted
    tail = jax.random.randint(keys_all[6], (OWNING_DEVICES, REQ_DEV), 1, PAGE_POSITIONS + 1)
    tail = jnp.where(long_slot | short_slot, PAGE_POSITIONS, tail)
    lengths = (page_list - 1) * PAGE_POSITIONS + tail
    return (to_next, to_prev, page_list, lengths)


def draw_movers(key, part):
    to_next, to_prev, page_list, lengths = layout(key)
    return jnp.stack([to_next, to_prev], axis=1).astype(jnp.int32)


def draw_cache_lengths(key, part):
    to_next, to_prev, page_list, lengths = layout(key)
    return lengths.reshape(TOTAL_REQUESTS).astype(jnp.int32)


def draw_page_table(key, part):
    to_next, to_prev, page_list, lengths = layout(key)
    table_key = jax.random.fold_in(key, 23)
    key_perm, key_fill = jax.random.split(table_key)
    shuffles = jax.vmap(lambda single: jax.random.permutation(single, PAGES_PER_DEVICE))(jax.random.split(key_perm, OWNING_DEVICES))
    start = jnp.cumsum(page_list, axis=1) - page_list
    column = jnp.arange(MAXP, dtype=jnp.int32)[None, None, :]
    where_from = jnp.minimum(start[:, :, None] + column, PAGES_PER_DEVICE - 1).reshape(OWNING_DEVICES, REQ_DEV * MAXP)
    picked = jnp.take_along_axis(shuffles, where_from, axis=1).reshape(OWNING_DEVICES, REQ_DEV, MAXP)
    filler = jax.random.randint(key_fill, (OWNING_DEVICES, REQ_DEV, MAXP), 0, PAGES_PER_DEVICE)
    table = jnp.where(column < page_list[:, :, None], picked, filler)
    return table.reshape(TOTAL_REQUESTS, MAXP).astype(jnp.int32)


def draw_queries(key, part):
    own_random_key = jax.random.fold_in(key, 41)
    value_rows = jnp.clip(jax.random.normal(own_random_key, (TOTAL_REQUESTS, NEW_TOKENS, QUERY_HEADS * HEAD_SIZE), jnp.float32), -6.0, 6.0)
    return value_rows.astype(jnp.bfloat16)


def draw_fresh_kv(key, part):
    own_random_key = jax.random.fold_in(key, 43)
    value_rows = jnp.clip(jax.random.normal(own_random_key, (TOTAL_REQUESTS, NEW_TOKENS, KEY_VALUE_HEADS, 2, HEAD_SIZE), jnp.float32), -6.0, 6.0)
    return value_rows.reshape(TOTAL_REQUESTS, NEW_TOKENS, KEY_VALUE_HEADS * 2 * HEAD_SIZE).astype(jnp.bfloat16)


def block_scale(own_key, shape, shards, low, largest):
    loudness, own = 1.0, jax.random.fold_in(own_key, 6)
    for axis_at, blocks in shards:
        heights = jnp.exp(jax.random.uniform(jax.random.fold_in(own, axis_at), (blocks,), jnp.float32, low / len(shards), largest / len(shards)))
        loudness = loudness * jnp.repeat(heights, shape[axis_at] // blocks).reshape([-1 if axis == axis_at else 1 for axis in range(len(shape))])
    return loudness


def normal_values(own_key, shape, spread, bound, cuts=(), held_as=jnp.bfloat16):
    level = block_scale(own_key, shape, cuts, -0.22, 0.18) if cuts else 1.0
    values = jax.random.normal(own_key, shape, jnp.float32) * spread * level
    return jnp.minimum(jnp.maximum(values, -bound), bound).astype(held_as)


def setup_inputs(seed: int = 0) -> dict:
    streams_of = jax.random.split(jax.random.key(seed), 8)
    return {
        "queries": draw_queries(jax.random.fold_in(streams_of[7], 71), 0),
        "fresh_kv": draw_fresh_kv(jax.random.fold_in(streams_of[7], 71), 0),
        "key_value_pages": normal_values(streams_of[2], (OWNING_DEVICES * PAGES_PER_DEVICE, PAGE_POSITIONS, KEY_VALUE_HEADS * 2 * HEAD_SIZE), 1.0, 6.0, ((0, 16), (2, 2))),
        "cache_lengths": draw_cache_lengths(jax.random.fold_in(streams_of[7], 71), 0),
        "page_table": draw_page_table(jax.random.fold_in(streams_of[7], 71), 0),
        "movers": draw_movers(jax.random.fold_in(streams_of[7], 71), 0),
        "w_out": normal_values(streams_of[6], (DOUT, QUERY_HEADS * HEAD_SIZE), (QUERY_HEADS * HEAD_SIZE) ** -0.5, 0.0625, ((0, 16), (1, 2))),
    }


masked_score = -1e30


def attend_one(query_rows, fresh_rows, page_list, length):
    cached_rows = MAXP * PAGE_POSITIONS
    query_head_rows = query_rows.astype(jnp.float32).reshape(NEW_TOKENS, KEY_VALUE_HEADS, QUERY_HEADS // KEY_VALUE_HEADS, HEAD_SIZE)
    cache_block = page_list.astype(jnp.float32).reshape(cached_rows, KEY_VALUE_HEADS, 2, HEAD_SIZE)
    newer_rows = fresh_rows.astype(jnp.float32).reshape(NEW_TOKENS, KEY_VALUE_HEADS, 2, HEAD_SIZE)
    all_keys = jnp.concatenate([cache_block[:, :, 0], newer_rows[:, :, 0]], axis=0)
    all_values = jnp.concatenate([cache_block[:, :, 1], newer_rows[:, :, 1]], axis=0)
    scores = jnp.einsum("qkgd,ckd->kgqc", query_head_rows, all_keys) * (HEAD_SIZE ** -0.5)
    position = jnp.arange(cached_rows + NEW_TOKENS, dtype=jnp.int32)[None, :]
    token_row = jnp.arange(NEW_TOKENS, dtype=jnp.int32)[:, None]
    valid = jnp.where(position < cached_rows, position < length, position - cached_rows <= token_row)
    scores = jnp.where(valid, scores, masked_score)
    highest = jnp.max(scores, axis=-1, keepdims=True)
    powers = jnp.exp(scores - highest)
    weights = (powers / jnp.sum(powers, axis=-1, keepdims=True)).astype(jnp.bfloat16)
    mixed = jnp.einsum("kgqc,ckd->qkgd", weights.astype(jnp.float32), all_values)
    return mixed.astype(jnp.bfloat16).reshape(NEW_TOKENS, QUERY_HEADS * HEAD_SIZE)


def pick_slot(grid, slot_index):
    return jnp.take_along_axis(grid, slot_index[:, None, None, None], axis=1)[:, 0]


def reference(queries, fresh_kv, key_value_pages, cache_lengths, page_table, movers, w_out):
    owner = jnp.arange(TOTAL_REQUESTS, dtype=jnp.int32) // REQ_DEV

    def single(request):
        page_rows = owner[request] * PAGES_PER_DEVICE + page_table[request]
        page_list = jnp.take(key_value_pages, page_rows, axis=0)
        return attend_one(queries[request], fresh_kv[request], page_list, cache_lengths[request])

    attended = lax.map(single, jnp.arange(TOTAL_REQUESTS, dtype=jnp.int32))
    grid = attended.reshape(OWNING_DEVICES, REQ_DEV, NEW_TOKENS, QUERY_HEADS * HEAD_SIZE)
    to_next = movers[:, 0]
    to_prev = movers[:, 1]
    from_left = jnp.roll(pick_slot(grid, to_next), 1, axis=0)
    from_right = jnp.roll(pick_slot(grid, to_prev), -1, axis=0)
    slot_ids = jnp.arange(REQ_DEV, dtype=jnp.int32)[None, :, None, None]
    placed = jnp.where(slot_ids == to_next[:, None, None, None], from_left[:, None],
                       jnp.where(slot_ids == to_prev[:, None, None, None], from_right[:, None], grid))
    flat = placed.reshape(TOKENS, QUERY_HEADS * HEAD_SIZE)
    return jnp.dot(flat, w_out.T, preferred_element_type=jnp.float32).astype(jnp.bfloat16)
```

```python
import functools

import jax
import jax.numpy as jnp
from jax import lax
from jax.experimental import pallas as pl
from jax.experimental.pallas import tpu as pltpu
from jax.sharding import PartitionSpec as P

HEAD_SIZE = 128
PAGE_GROUP = 8
LOG2E = 1.4426950408889634
MASKED = -1e30


def passed_along(block, axis, distance):
    devices = range(lax.axis_size(axis))
    route = [((i - distance) % len(devices), i) for i in devices]
    return lax.ppermute(block, axis, route)


def nt(a, b):
    return lax.dot_general(a, b, (((1,), (1,)), ((), ())), preferred_element_type=jnp.float32)


def attend_kernel(kv_heads, group, len_ref, tab_ref, order_ref, q_ref, f_ref, pages_ref, o_ref, qs, ms, ls, acc):
    slot = order_ref[pl.program_id(0)]
    tokens = q_ref.shape[1]
    page = pages_ref.shape[1]
    rows = group * tokens
    maxp = tab_ref.shape[1]
    length = len_ref[slot]
    factor = HEAD_SIZE ** (-0.5) * LOG2E
    span = PAGE_GROUP * page
    groups = (length + span - 1) // span
    token = lax.broadcasted_iota(jnp.int32, (rows, tokens), 0) % tokens
    newer = lax.broadcasted_iota(jnp.int32, (rows, tokens), 1)
    for g in range(kv_heads):
        heads = [
            q_ref[0, :, (g * group + h) * HEAD_SIZE : (g * group + h + 1) * HEAD_SIZE].astype(jnp.float32)
            for h in range(group)
        ]
        q = jnp.concatenate(heads, axis=0).astype(jnp.bfloat16)
        qs[g] = q
        key = f_ref[0, :, 2 * g * HEAD_SIZE : (2 * g + 1) * HEAD_SIZE]
        value = f_ref[0, :, (2 * g + 1) * HEAD_SIZE : (2 * g + 2) * HEAD_SIZE]
        s = jnp.where(newer <= token, nt(q, key), MASKED)
        m = jnp.max(s, axis=-1, keepdims=True)
        p = jnp.exp2((s - m) * factor)
        ms[g] = m
        ls[g] = jnp.sum(p, axis=-1, keepdims=True)
        acc[g] = jnp.dot(p.astype(jnp.bfloat16), value, preferred_element_type=jnp.float32)

    def body(at, carry):
        ids = [tab_ref[slot, jnp.minimum(at * PAGE_GROUP + u, maxp - 1)] for u in range(PAGE_GROUP)]
        pos = at * span + lax.broadcasted_iota(jnp.int32, (rows, span), 1)
        valid = pos < length
        def side(g, which):
            first = (2 * g + which) * HEAD_SIZE
            return jnp.concatenate([pages_ref[i, :, first : first + HEAD_SIZE] for i in ids], axis=0)

        def scored(g):
            return jnp.where(valid, nt(qs[g], side(g, 0)), MASKED)

        s = scored(0)
        for g in range(kv_heads):
            following = scored(g + 1) if g + 1 < kv_heads else None
            before = ms[g]
            m = jnp.maximum(before, jnp.max(s, axis=-1, keepdims=True))
            fade = jnp.exp2((before - m) * factor)
            p = jnp.exp2((s - m) * factor)
            ms[g] = m
            ls[g] = ls[g] * fade + jnp.sum(p, axis=-1, keepdims=True)
            acc[g] = acc[g] * fade + jnp.dot(
                p.astype(jnp.bfloat16), side(g, 1), preferred_element_type=jnp.float32
            )
            s = following
        return carry

    lax.fori_loop(0, groups, body, 0)
    for g in range(kv_heads):
        o = acc[g] / ls[g]
        for h in range(group):
            o_ref[0, :, (g * group + h) * HEAD_SIZE : (g * group + h + 1) * HEAD_SIZE] = o[
                h * tokens : (h + 1) * tokens
            ].astype(jnp.bfloat16)


def attend(queries, fresh_kv, pages, lengths, table, order):
    slots, tokens, width = queries.shape
    kv_heads = fresh_kv.shape[2] // (2 * HEAD_SIZE)
    group = width // (kv_heads * HEAD_SIZE)
    rows = group * tokens
    return pl.pallas_call(
        functools.partial(attend_kernel, kv_heads, group),
        out_shape=jax.ShapeDtypeStruct(queries.shape, jnp.bfloat16),
        grid_spec=pltpu.PrefetchScalarGridSpec(
            num_scalar_prefetch=3,
            grid=(slots,),
            in_specs=[
                pl.BlockSpec((1, tokens, width), lambda s, a, b, o: (o[s], 0, 0)),
                pl.BlockSpec((1, tokens, fresh_kv.shape[2]), lambda s, a, b, o: (o[s], 0, 0)),
                pl.BlockSpec(pages.shape, lambda s, a, b, o: (0, 0, 0), pipeline_mode=pl.Buffered(1)),
            ],
            out_specs=pl.BlockSpec((1, tokens, width), lambda s, a, b, o: (s, 0, 0)),
            scratch_shapes=[
                pltpu.VMEM((kv_heads, rows, HEAD_SIZE), jnp.bfloat16),
                pltpu.VMEM((kv_heads, rows, 1), jnp.float32),
                pltpu.VMEM((kv_heads, rows, 1), jnp.float32),
                pltpu.VMEM((kv_heads, rows, HEAD_SIZE), jnp.float32),
            ],
        ),
        compiler_params=pltpu.CompilerParams(vmem_limit_bytes=40 << 20),
        cost_estimate=pl.CostEstimate(
            flops=4 * rows * kv_heads * pages.shape[0] * pages.shape[1] * HEAD_SIZE,
            transcendentals=rows * kv_heads * pages.shape[0] * pages.shape[1],
            bytes_accessed=pages.size * 2 + queries.size * 4,
        ),
    )(lengths, table, order, queries, fresh_kv, pages)

MESH = pl.DeviceIdType.MESH
GROUPS = 3
WCH = 2


def project_kernel(
    att_ref, w_ref, o_ref, abuf, wbuf, psend, precv, ploc, csum0, csum, obuf0, obuf,
    wl_sem, wz_send, wz_recv, wt_send, wt_recv, a1_send, a2_send, f_send, az_recv, ay_recv,
    x_send, x_recv, o_send0, o_send, o_recv0, o_recv,
):
    me, x = lax.axis_index("req"), lax.axis_index("tp")
    n = 16
    z, y, c = me // 4, (me // 2) % 2, me % 2
    own = z % 2
    oth = 1 - own
    t = z // 2
    inner = jnp.logical_or(z == 1, z == 2)
    outer = jnp.logical_not(inner)
    far = 2 - t
    zp = z + 1 - 2 * own
    keeper = x == t
    mine = 2 * own + y
    rows = att_ref.shape[1]
    wide = w_ref.shape[0]
    wrows = wide // WCH

    def at(zz, yy, cc, xx):
        return {"req": zz * 4 + yy * 2 + cc, "tp": xx}

    def remote(src, dst, ss, rs, dev):
        return pltpu.make_async_remote_copy(
            src_ref=src, dst_ref=dst, send_sem=ss, recv_sem=rs, device_id=dev, device_id_type=MESH
        )

    barrier = pltpu.get_barrier_semaphore()
    my_index = me * 2 + x

    def greet(i, carry):
        target = (my_index + i) % (2 * n)
        pl.semaphore_signal(
            barrier, inc=1, device_id={"req": target // 2, "tp": target % 2}, device_id_type=MESH
        )
        return carry

    lax.fori_loop(1, 2 * n, greet, 0)

    local_w = pltpu.make_async_copy(w_ref, wbuf.at[own, c], wl_sem)
    local_w.start()
    pl.semaphore_wait(barrier, 2 * n - 1)

    def wz(i):
        piece = pl.ds(i * wrows, wrows)
        return remote(w_ref.at[piece], wbuf.at[own, c, piece], wz_send.at[i], wz_recv.at[i], at(zp, y, c, x))

    def wz_in(i):
        piece = pl.ds(i * wrows, wrows)
        return remote(w_ref.at[piece], wbuf.at[oth, c, piece], wz_send.at[i], wz_recv.at[i], at(zp, y, c, x))

    def wt_own():
        return remote(w_ref, wbuf.at[own, c], wt_send.at[WCH], wt_recv.at[WCH], at(z, y, 1 - c, x))

    def wt_own_in():
        return remote(w_ref, wbuf.at[own, 1 - c], wt_send.at[WCH], wt_recv.at[WCH], at(z, y, 1 - c, x))

    def wt(i):
        where = wbuf.at[oth, c, pl.ds(i * wrows, wrows)]
        return remote(where, where, wt_send.at[i], wt_recv.at[i], at(z, y, 1 - c, x))

    def wt_in(i):
        where = wbuf.at[oth, 1 - c, pl.ds(i * wrows, wrows)]
        return remote(where, where, wt_send.at[i], wt_recv.at[i], at(z, y, 1 - c, x))

    def a1_outer(g):
        return remote(att_ref.at[g], abuf.at[g, mine], a1_send.at[g], ay_recv.at[g, own], at(z, 1 - y, c, x))

    def a1_inner(g):
        return remote(att_ref.at[g], abuf.at[g, mine], a1_send.at[g], az_recv.at[g, own], at(zp, y, c, x))

    def a2(g):
        return remote(att_ref.at[g], abuf.at[g, mine], a2_send.at[g], az_recv.at[g, own], at(far, y, c, x))

    def z_in(g, q):
        where = abuf.at[g, 2 * q + y]
        return remote(att_ref.at[g], where, a1_send.at[g], az_recv.at[g, q], at(zp, y, c, x))

    def forward(g, q):
        where = abuf.at[g, 2 * q + y]
        return remote(where, where, f_send.at[g, q], ay_recv.at[g, q], at(z, 1 - y, c, x))

    def y_in(g, q):
        where = abuf.at[g, 2 * q + 1 - y]
        return remote(where, where, f_send.at[g, q], ay_recv.at[g, q], at(z, 1 - y, c, x))

    def send_rows(g):
        a2(g).start()

        @pl.when(inner)
        def _():
            a1_inner(g).start()

        @pl.when(outer)
        def _():
            a1_outer(g).start()
            abuf[g, mine] = att_ref[g]

    def pass_on(g):
        z_in(g, oth).wait_recv()
        forward(g, oth).start()

        @pl.when(inner)
        def _():
            z_in(g, own).wait_recv()
            forward(g, own).start()

    def x_copy(g, f):
        return remote(psend.at[g, f], precv.at[g, f], x_send.at[g, f], x_recv.at[g, f], at(z, y, c, 1 - x))

    def compute(g, f):
        a = abuf[g].reshape(4 * rows, abuf.shape[3])
        for cc in range(2):
            part = nt(a, wbuf[f, cc])

            @pl.when(keeper)
            def _():
                ploc[g, f, :, cc * wide : (cc + 1) * wide] = part

            @pl.when(jnp.logical_not(keeper))
            def _():
                psend[g, f, :, cc * wide : (cc + 1) * wide] = part.astype(jnp.bfloat16)

        @pl.when(jnp.logical_not(keeper))
        def _():
            x_copy(g, f).start()

    def out0(j, s, f):
        r = (2 * own + s // 2) * 4 + (s % 2) * 2 + c
        dest = (r + n + 1 - 2 * j) % n
        return remote(
            csum0.at[j, s, f], obuf0.at[j, y, f], o_send0.at[j, s, f], o_recv0.at[j, y, f], {"req": dest, "tp": x}
        )

    def out(g, s, f):
        return remote(
            csum.at[g - 1, s, f], obuf.at[g - 1, y, f], o_send.at[g - 1, s, f], o_recv.at[g - 1, y, f],
            at(2 * own + s // 2, s % 2, c, x),
        )

    def is_self(s):
        return jnp.logical_and(outer, s == mine)

    half = rows // 2

    def reduce(g, f):
        @pl.when(keeper)
        def _():
            x_copy(g, f).wait_recv()

            def one(s, carry):
                base = pl.multiple_of(s * rows, rows)
                total = ploc[g, f, pl.ds(base, rows)] + precv[g, f, pl.ds(base, rows)].astype(jnp.float32)

                @pl.when(g == 0)
                def _():
                    for j in range(2):
                        csum0[j, s, f] = total[j * half : (j + 1) * half].astype(jnp.bfloat16)
                        out0(j, s, f).start()

                @pl.when(g > 0)
                def _():
                    for j in range(2):
                        csum[g - 1, s, f, j] = total[j * half : (j + 1) * half].astype(jnp.bfloat16)

                    @pl.when(is_self(s))
                    def _():
                        obuf[g - 1, y, f] = csum[g - 1, s, f]

                    @pl.when(jnp.logical_not(is_self(s)))
                    def _():
                        out(g, s, f).start()

                return carry

            lax.fori_loop(0, 4, one, 0)

    for g in range(GROUPS):
        send_rows(g)
    for i in range(WCH):
        wz(i).start()
    wt_own().start()
    local_w.wait()
    wt_own_in().wait_recv()

    pass_on(0)

    def first(g, carry):
        @pl.when(g < GROUPS - 1)
        def _():
            pass_on(g + 1)

        for q in range(2):
            y_in(g, q).wait_recv()
        compute(g, own)

        @pl.when(g >= 1)
        def _():
            reduce(g - 1, own)

        return carry

    lax.fori_loop(0, GROUPS, first, 0)
    for i in range(WCH):
        wz_in(i).wait_recv()
        wt(i).start()
    for i in range(WCH):
        wt_in(i).wait_recv()

    def second(g, carry):
        compute(g, oth)
        reduce((g + GROUPS - 1) % GROUPS, jnp.where(g == 0, own, oth))
        return carry

    lax.fori_loop(0, GROUPS, second, 0)
    reduce(GROUPS - 1, oth)

    for i in range(WCH):
        wz(i).wait_send()
        wt(i).wait_send()
    wt_own().wait_send()

    def sent(g, carry):
        a2(g).wait_send()
        a1_inner(g).wait_send()
        forward(g, oth).wait_send()

        @pl.when(inner)
        def _():
            forward(g, own).wait_send()

        for f in range(2):
            @pl.when(jnp.logical_not(keeper))
            def _():
                x_copy(g, f).wait_send()

            @pl.when(keeper)
            def _():
                def gone(s, carry):
                    @pl.when(g == 0)
                    def _():
                        for j in range(2):
                            out0(j, s, f).wait_send()

                    @pl.when(jnp.logical_and(g > 0, jnp.logical_not(is_self(s))))
                    def _():
                        out(g, s, f).wait_send()

                    return carry

                lax.fori_loop(0, 4, gone, 0)
        return carry

    lax.fori_loop(0, GROUPS, sent, 0)

    for yy in range(2):
        for f in range(2):
            cols = slice(f * 4 * wide + yy * 2 * wide, f * 4 * wide + (yy + 1) * 2 * wide)
            for j in range(2):
                remote(csum0.at[0, 0, 0], obuf0.at[j, yy, f], o_send0.at[0, 0, 0], o_recv0.at[j, yy, f], at(z, y, 1 - c, x)).wait_recv()
                o_ref[j, :, cols] = obuf0[j, yy, f]
            for g in range(1, GROUPS):
                @pl.when(jnp.logical_not(jnp.logical_and(jnp.logical_and(keeper, outer), y == yy)))
                def _():
                    remote(csum.at[0, 0, 0], obuf.at[g - 1, yy, f], o_send.at[0, 0, 0], o_recv.at[g - 1, yy, f], at(z, y, 1 - c, x)).wait_recv()

                for j in range(2):
                    o_ref[2 * g + j, :, cols] = obuf[g - 1, yy, f, j]


def project(att, w_out):
    slots, tokens, width = att.shape
    rows = slots * tokens // GROUPS
    wide = w_out.shape[0]
    dma = pltpu.SemaphoreType.DMA
    vmem = pl.BlockSpec(memory_space=pltpu.VMEM)
    b = jnp.bfloat16
    return pl.pallas_call(
        project_kernel,
        out_shape=jax.ShapeDtypeStruct((slots, tokens, 8 * wide), b),
        in_specs=[vmem, pl.BlockSpec(memory_space=pl.ANY)],
        out_specs=vmem,
        scratch_shapes=[
            pltpu.VMEM((GROUPS, 4, rows, width), b),
            pltpu.VMEM((2, 2, wide, width), b),
            pltpu.VMEM((GROUPS, 2, 4 * rows, 2 * wide), b),
            pltpu.VMEM((GROUPS, 2, 4 * rows, 2 * wide), b),
            pltpu.VMEM((GROUPS, 2, 4 * rows, 2 * wide), jnp.float32),
            pltpu.VMEM((2, 4, 2, tokens, 2 * wide), b),
            pltpu.VMEM((GROUPS - 1, 4, 2, 2, tokens, 2 * wide), b),
            pltpu.VMEM((2, 2, 2, tokens, 2 * wide), b),
            pltpu.VMEM((GROUPS - 1, 2, 2, 2, tokens, 2 * wide), b),
            dma, dma((WCH,)), dma((WCH,)), dma((WCH + 1,)), dma((WCH + 1,)),
            dma((GROUPS,)), dma((GROUPS,)), dma((GROUPS, 2)), dma((GROUPS, 2)), dma((GROUPS, 2)),
            dma((GROUPS, 2)), dma((GROUPS, 2)),
            dma((2, 4, 2)), dma((GROUPS - 1, 4, 2)), dma((2, 2, 2)), dma((GROUPS - 1, 2, 2)),
        ],
        compiler_params=pltpu.CompilerParams(
            collective_id=0, has_side_effects=True, vmem_limit_bytes=48 << 20
        ),
    )(att.reshape(GROUPS, rows, width), w_out)


def per_device(queries, fresh_kv, key_value_pages, cache_lengths, page_table, movers, w_out):
    slots, tokens, width = queries.shape
    to_next = movers[0, 0]
    to_prev = movers[0, 1]
    if lax.axis_size("tp") == 2 and lax.axis_size("req") == 16 and slots == 2 * GROUPS:
        slot_ids = jnp.arange(slots, dtype=jnp.int32)
        key = jnp.where(slot_ids == to_next, -2, jnp.where(slot_ids == to_prev, -1, slot_ids))
        rank = jnp.sum((key[None, :] < key[:, None]).astype(jnp.int32), axis=1)
        order = jnp.sum(jnp.where(rank[None, :] == slot_ids[:, None], slot_ids[None, :], 0), axis=1)
        attended = attend(queries, fresh_kv, key_value_pages, cache_lengths, page_table, order)
        done = project(attended, w_out)
        return jnp.take(done, rank, axis=0, mode="clip").reshape(slots * tokens, -1)
    order = jnp.arange(slots, dtype=jnp.int32)
    attended = attend(queries, fresh_kv, key_value_pages, cache_lengths, page_table, order)
    from_left = passed_along(attended[to_next], "req", 1)
    from_right = passed_along(attended[to_prev], "req", -1)
    slot_ids = jnp.arange(slots, dtype=jnp.int32)[:, None, None]
    placed = jnp.where(
        slot_ids == to_next, from_left[None], jnp.where(slot_ids == to_prev, from_right[None], attended)
    )
    flat = placed.reshape(slots * tokens, width)
    partial_sum = lax.dot_general(
        flat,
        lax.all_gather(w_out, "req", axis=0, tiled=True),
        (((1,), (1,)), ((), ())),
        preferred_element_type=jnp.float32,
    )
    return lax.psum_scatter(partial_sum, "tp", scatter_dimension=1, tiled=True).astype(jnp.bfloat16)


def solution(mesh):
    return jax.shard_map(
        per_device,
        mesh=mesh,
        in_specs=(
            P("req", None, "tp"),
            P("req", None, "tp"),
            P("req", None, "tp"),
            P("req"),
            P("req", None),
            P("req", None),
            P("req", "tp"),
        ),
        out_specs=P("req", "tp"),
        check_vma=False,
    )
```

```python
import functools

import jax
import jax.numpy as jnp
from jax import lax
from jax.experimental import pallas as pl
from jax.experimental.pallas import tpu as pltpu
from jax.sharding import PartitionSpec as P

HEAD_SIZE = 128
PAGE_GROUP = 8
LOG2E = 1.4426950408889634
MASKED = -1e30


def passed_along(block, axis, distance):
    devices = range(lax.axis_size(axis))
    route = [((i - distance) % len(devices), i) for i in devices]
    return lax.ppermute(block, axis, route)


def nt(a, b):
    return lax.dot_general(a, b, (((1,), (1,)), ((), ())), preferred_element_type=jnp.float32)


def attend_kernel(kv_heads, group, len_ref, tab_ref, q_ref, f_ref, pages_ref, o_ref, qs, ms, ls, acc):
    slot = pl.program_id(0)
    tokens = q_ref.shape[1]
    page = pages_ref.shape[1]
    rows = group * tokens
    maxp = tab_ref.shape[1]
    length = len_ref[slot]
    factor = HEAD_SIZE ** (-0.5) * LOG2E
    span = PAGE_GROUP * page
    groups = (length + span - 1) // span
    token = lax.broadcasted_iota(jnp.int32, (rows, tokens), 0) % tokens
    newer = lax.broadcasted_iota(jnp.int32, (rows, tokens), 1)
    for g in range(kv_heads):
        heads = [
            q_ref[0, :, (g * group + h) * HEAD_SIZE : (g * group + h + 1) * HEAD_SIZE].astype(jnp.float32)
            for h in range(group)
        ]
        q = jnp.concatenate(heads, axis=0).astype(jnp.bfloat16)
        qs[g] = q
        key = f_ref[0, :, 2 * g * HEAD_SIZE : (2 * g + 1) * HEAD_SIZE]
        value = f_ref[0, :, (2 * g + 1) * HEAD_SIZE : (2 * g + 2) * HEAD_SIZE]
        s = jnp.where(newer <= token, nt(q, key), MASKED)
        m = jnp.max(s, axis=-1, keepdims=True)
        p = jnp.exp2((s - m) * factor)
        ms[g] = m
        ls[g] = jnp.sum(p, axis=-1, keepdims=True)
        acc[g] = jnp.dot(p.astype(jnp.bfloat16), value, preferred_element_type=jnp.float32)

    def body(at, carry):
        ids = [tab_ref[slot, jnp.minimum(at * PAGE_GROUP + u, maxp - 1)] for u in range(PAGE_GROUP)]
        pos = at * span + lax.broadcasted_iota(jnp.int32, (rows, span), 1)
        valid = pos < length
        def side(g, which):
            first = (2 * g + which) * HEAD_SIZE
            return jnp.concatenate([pages_ref[i, :, first : first + HEAD_SIZE] for i in ids], axis=0)

        def scored(g):
            return jnp.where(valid, nt(qs[g], side(g, 0)), MASKED)

        s = scored(0)
        for g in range(kv_heads):
            following = scored(g + 1) if g + 1 < kv_heads else None
            before = ms[g]
            m = jnp.maximum(before, jnp.max(s, axis=-1, keepdims=True))
            fade = jnp.exp2((before - m) * factor)
            p = jnp.exp2((s - m) * factor)
            ms[g] = m
            ls[g] = ls[g] * fade + jnp.sum(p, axis=-1, keepdims=True)
            acc[g] = acc[g] * fade + jnp.dot(
                p.astype(jnp.bfloat16), side(g, 1), preferred_element_type=jnp.float32
            )
            s = following
        return carry

    lax.fori_loop(0, groups, body, 0)
    for g in range(kv_heads):
        o = acc[g] / ls[g]
        for h in range(group):
            o_ref[0, :, (g * group + h) * HEAD_SIZE : (g * group + h + 1) * HEAD_SIZE] = o[
                h * tokens : (h + 1) * tokens
            ].astype(jnp.bfloat16)


def attend(queries, fresh_kv, pages, lengths, table):
    slots, tokens, width = queries.shape
    kv_heads = fresh_kv.shape[2] // (2 * HEAD_SIZE)
    group = width // (kv_heads * HEAD_SIZE)
    rows = group * tokens
    return pl.pallas_call(
        functools.partial(attend_kernel, kv_heads, group),
        out_shape=jax.ShapeDtypeStruct(queries.shape, jnp.bfloat16),
        grid_spec=pltpu.PrefetchScalarGridSpec(
            num_scalar_prefetch=2,
            grid=(slots,),
            in_specs=[
                pl.BlockSpec((1, tokens, width), lambda s, a, b: (s, 0, 0)),
                pl.BlockSpec((1, tokens, fresh_kv.shape[2]), lambda s, a, b: (s, 0, 0)),
                pl.BlockSpec(pages.shape, lambda s, a, b: (0, 0, 0), pipeline_mode=pl.Buffered(1)),
            ],
            out_specs=pl.BlockSpec((1, tokens, width), lambda s, a, b: (s, 0, 0)),
            scratch_shapes=[
                pltpu.VMEM((kv_heads, rows, HEAD_SIZE), jnp.bfloat16),
                pltpu.VMEM((kv_heads, rows, 1), jnp.float32),
                pltpu.VMEM((kv_heads, rows, 1), jnp.float32),
                pltpu.VMEM((kv_heads, rows, HEAD_SIZE), jnp.float32),
            ],
        ),
        compiler_params=pltpu.CompilerParams(vmem_limit_bytes=40 << 20),
        cost_estimate=pl.CostEstimate(
            flops=4 * rows * kv_heads * pages.shape[0] * pages.shape[1] * HEAD_SIZE,
            transcendentals=rows * kv_heads * pages.shape[0] * pages.shape[1],
            bytes_accessed=pages.size * 2 + queries.size * 4,
        ),
    )(lengths, table, queries, fresh_kv, pages)

MESH = pl.DeviceIdType.MESH
GROUPS = 3
HALVES = 2
PIECES = 6
AHEAD = 2
UNITS = 12
LAG = 2
STEP_PAGES = 4
MOVER_POSITIONS = 512
UNIT_G = (0, 0, 1, 1, 0, 1, 0, 1, 2, 2, 2, 2)
UNIT_F = (0, 0, 0, 0, 1, 1, 1, 1, 0, 0, 1, 1)
UNIT_I = (0, 1, 0, 1, 0, 0, 1, 1, 0, 1, 0, 1)


def pick(at, table):
    value = table[0]
    for k in range(1, len(table)):
        if table[k] != table[k - 1]:
            value = jnp.where(at >= k, table[k], value)
    return value


def fused_kernel(
    rank_steps,
    q_any, f_any, pages_any, len_ref, tab_ref, mov_ref, w_ref, o_ref,
    q_ref, f_ref, pages_ref, order_ref, qs, ms, ls, acc, att_ref,
    abuf, wbuf, psend, precv, ploc, csum, obuf,
    in_sem, wl_sem, wz_send, wz_recv, wt_send, wt_recv, a1_send, a2_send, f_send, az_recv, ay_recv,
    x_send, x_recv, o_send0, o_send, o_recv0, o_recv,
):
    me, x = lax.axis_index("req"), lax.axis_index("tp")
    n = 16
    z, y, c = me // 4, (me // 2) % 2, me % 2
    own = z % 2
    oth = 1 - own
    t = z // 2
    inner = jnp.logical_or(z == 1, z == 2)
    outer = jnp.logical_not(inner)
    far = 2 - t
    zp = z + 1 - 2 * own
    keeper = x == t
    mine = 2 * own + y
    rows = att_ref.shape[1]
    slots, tokens = q_ref.shape[0], q_ref.shape[1]
    kv_heads, group = qs.shape[0], qs.shape[1] // q_ref.shape[1]
    page = pages_ref.shape[1]
    maxp = tab_ref.shape[1]
    qrows = group * tokens
    factor = HEAD_SIZE ** (-0.5) * LOG2E
    wide = w_ref.shape[0]
    wrows = wide // 2
    cols = att_ref.shape[2] // HALVES

    def at(zz, yy, cc, xx):
        return {"req": zz * 4 + yy * 2 + cc, "tp": xx}

    def remote(src, dst, ss, rs, dev):
        return pltpu.make_async_remote_copy(
            src_ref=src, dst_ref=dst, send_sem=ss, recv_sem=rs, device_id=dev, device_id_type=MESH
        )

    barrier = pltpu.get_barrier_semaphore()
    my_index = me * 2 + x

    def greet(i, carry):
        target = (my_index + i) % (2 * n)
        pl.semaphore_signal(
            barrier, inc=1, device_id={"req": target // 2, "tp": target % 2}, device_id_type=MESH
        )
        return carry

    lax.fori_loop(1, 2 * n, greet, 0)

    def local_w(i):
        return pltpu.make_async_copy(w_ref.at[pl.ds(i * wrows, wrows)], wbuf.at[own, i, c], wl_sem.at[i])

    inputs = [
        pltpu.make_async_copy(q_any, q_ref, in_sem.at[0]),
        pltpu.make_async_copy(f_any, f_ref, in_sem.at[1]),
        pltpu.make_async_copy(pages_any, pages_ref, in_sem.at[2]),
    ]
    for copy in inputs:
        copy.start()
    for i in range(2):
        local_w(i).start()

    keys = []
    for slot in range(slots):
        key = len_ref[slot] * slots + slot
        key = jnp.where(mov_ref[0, 1] == slot, -1, key)
        keys.append(jnp.where(mov_ref[0, 0] == slot, -2, key))
    ranks = []
    for slot in range(slots):
        rank = 0
        for i in range(slots):
            if i != slot:
                rank = rank + jnp.where(keys[i] < keys[slot], 1, 0)
        ranks.append(rank)
    for k in range(slots):
        slot_at = 0
        for slot in range(1, slots):
            slot_at = slot_at + jnp.where(ranks[slot] == k, slot, 0)
        order_ref[k] = slot_at
        order_ref[slots + k] = ranks[k]
    pl.semaphore_wait(barrier, 2 * n - 1)

    def wz(i):
        return remote(
            w_ref.at[pl.ds(i * wrows, wrows)], wbuf.at[own, i, c], wz_send.at[i], wz_recv.at[i], at(zp, y, c, x)
        )

    def wz_in(i):
        return remote(
            w_ref.at[pl.ds(i * wrows, wrows)], wbuf.at[oth, i, c], wz_send.at[i], wz_recv.at[i], at(zp, y, c, x)
        )

    def twin(f, i):
        src = w_ref.at[pl.ds(i * wrows, wrows)] if f is own else wbuf.at[f, i, c]
        return remote(src, wbuf.at[f, i, c], wt_send.at[f, i], wt_recv.at[f, i], at(z, y, 1 - c, x))

    def twin_in(f, i):
        where = wbuf.at[f, i, 1 - c]
        return remote(where, where, wt_send.at[f, i], wt_recv.at[f, i], at(z, y, 1 - c, x))

    token = lax.broadcasted_iota(jnp.int32, (qrows, tokens), 0) % tokens
    newer = lax.broadcasted_iota(jnp.int32, (qrows, tokens), 1)
    span = STEP_PAGES * page

    def attend_rank(k):
        slot = order_ref[k]
        j = k % 2
        length = len_ref[slot]
        for g in range(kv_heads):
            heads = [
                q_ref[slot, :, (g * group + h) * HEAD_SIZE : (g * group + h + 1) * HEAD_SIZE].astype(jnp.float32)
                for h in range(group)
            ]
            q = jnp.concatenate(heads, axis=0).astype(jnp.bfloat16)
            qs[g] = q
            key = f_ref[slot, :, 2 * g * HEAD_SIZE : (2 * g + 1) * HEAD_SIZE]
            value = f_ref[slot, :, (2 * g + 1) * HEAD_SIZE : (2 * g + 2) * HEAD_SIZE]
            s = jnp.where(newer <= token, nt(q, key), MASKED)
            m = jnp.max(s, axis=-1, keepdims=True)
            p = jnp.exp2((s - m) * factor)
            ms[g] = m
            ls[j, g] = jnp.sum(p, axis=-1, keepdims=True)
            acc[j, g] = jnp.dot(p.astype(jnp.bfloat16), value, preferred_element_type=jnp.float32)

        def body(at_step, carry):
            ids = [tab_ref[slot, jnp.minimum(at_step * STEP_PAGES + u, maxp - 1)] for u in range(STEP_PAGES)]
            pos = at_step * span + lax.broadcasted_iota(jnp.int32, (qrows, span), 1)
            valid = pos < length

            def side(g, which):
                first = (2 * g + which) * HEAD_SIZE
                return jnp.concatenate([pages_ref[i, :, first : first + HEAD_SIZE] for i in ids], axis=0)

            def scored(g):
                return jnp.where(valid, nt(qs[g], side(g, 0)), MASKED)

            s = scored(0)
            for g in range(kv_heads):
                following = scored(g + 1) if g + 1 < kv_heads else None
                before = ms[g]
                m = jnp.maximum(before, jnp.max(s, axis=-1, keepdims=True))
                fade = jnp.exp2((before - m) * factor)
                p = jnp.exp2((s - m) * factor)
                ms[g] = m
                ls[j, g] = ls[j, g] * fade + jnp.sum(p, axis=-1, keepdims=True)
                acc[j, g] = acc[j, g] * fade + jnp.dot(
                    p.astype(jnp.bfloat16), side(g, 1), preferred_element_type=jnp.float32
                )
                s = following
            return carry

        lax.fori_loop(0, pick(k, rank_steps), body, 0)

    def finish_group(at_group):
        for g in range(kv_heads):
            o = [acc[j, g] / ls[j, g] for j in range(2)]
            for h in range(group):
                lane = (g * group + h) * HEAD_SIZE
                att_ref[at_group, :, lane : lane + HEAD_SIZE] = jnp.concatenate(
                    [o[j][h * tokens : (h + 1) * tokens] for j in range(2)], axis=0
                ).astype(jnp.bfloat16)

        @pl.when(outer)
        def _():
            abuf[at_group, mine] = att_ref[at_group]

    def rows_of(p):
        return att_ref.at[p // HALVES, :, pl.ds(pl.multiple_of((p % HALVES) * cols, cols), cols)]

    def place(p, s):
        return abuf.at[p // HALVES, s, :, pl.ds(pl.multiple_of((p % HALVES) * cols, cols), cols)]

    def a1_outer(p):
        return remote(rows_of(p), place(p, mine), a1_send.at[p], ay_recv.at[p, own], at(z, 1 - y, c, x))

    def a1_inner(p):
        return remote(rows_of(p), place(p, mine), a1_send.at[p], az_recv.at[p, own], at(zp, y, c, x))

    def a2(p):
        return remote(rows_of(p), place(p, mine), a2_send.at[p], az_recv.at[p, own], at(far, y, c, x))

    def z_in(p, q):
        where = place(p, 2 * q + y)
        return remote(where, where, a1_send.at[p], az_recv.at[p, q], at(zp, y, c, x))

    def forward(p, q):
        where = place(p, 2 * q + y)
        return remote(where, where, f_send.at[p, q], ay_recv.at[p, q], at(z, 1 - y, c, x))

    def y_in(p, q):
        where = place(p, 2 * q + 1 - y)
        return remote(where, where, f_send.at[p, q], ay_recv.at[p, q], at(z, 1 - y, c, x))

    def send_rows(p):
        a2(p).start()

        @pl.when(inner)
        def _():
            a1_inner(p).start()

        @pl.when(outer)
        def _():
            a1_outer(p).start()

    def rows_left(p):
        a2(p).wait_send()
        a1_inner(p).wait_send()

    def pass_on(p):
        z_in(p, oth).wait_recv()
        forward(p, oth).start()

        @pl.when(inner)
        def _():
            z_in(p, own).wait_recv()
            forward(p, own).start()

        @pl.when(p < PIECES - AHEAD)
        def _():
            rows_left(p)
            send_rows(p + AHEAD)

    def forwarded(g):
        def one(h, carry):
            for q in range(2):
                y_in(g * HALVES + h, q).wait_recv()
            return carry

        lax.fori_loop(0, HALVES, one, 0)

    def unit(u):
        f = pick(u, UNIT_F)
        return pick(u, UNIT_G), jnp.where(f == 0, own, oth), pick(u, UNIT_I)

    def x_copy(g, f, i):
        return remote(
            psend.at[g, f, i], precv.at[g, f, i], x_send.at[g, f, i], x_recv.at[g, f, i], at(z, y, c, 1 - x)
        )

    def compute(u):
        g, f, i = unit(u)
        a = abuf[g].reshape(4 * rows, abuf.shape[3])
        part = nt(a, wbuf[f, i].reshape(2 * wrows, wbuf.shape[4]))

        @pl.when(keeper)
        def _():
            ploc[g, f, i] = part

        @pl.when(jnp.logical_not(keeper))
        def _():
            psend[g, f, i] = part.astype(jnp.bfloat16)
            x_copy(g, f, i).start()

    def out0(j, s, f, i):
        r = (2 * own + s // 2) * 4 + (s % 2) * 2 + c
        dest = (r + n + 1 - 2 * j) % n
        return remote(
            csum.at[s, f, i, j], obuf.at[y, f, i, j], o_send0.at[j, s, f, i], o_recv0.at[j, y, f, i],
            {"req": dest, "tp": x},
        )

    def out(g, s, f, i):
        pair = pl.ds(2 * g, 2)
        return remote(
            csum.at[s, f, i, pair], obuf.at[y, f, i, pair], o_send.at[g - 1, s, f, i],
            o_recv.at[g - 1, y, f, i], at(2 * own + s // 2, s % 2, c, x),
        )

    def is_self(s):
        return jnp.logical_and(outer, s == mine)

    half = rows // 2

    def reduce(u):
        g, f, i = unit(u)

        @pl.when(keeper)
        def _():
            x_copy(g, f, i).wait_recv()

            def one(s, carry):
                base = pl.multiple_of(s * rows, rows)
                total = ploc[g, f, i, pl.ds(base, rows)] + precv[g, f, i, pl.ds(base, rows)].astype(jnp.float32)

                @pl.when(g == 0)
                def _():
                    for j in range(2):
                        csum[s, f, i, j] = total[j * half : (j + 1) * half].astype(jnp.bfloat16)
                        out0(j, s, f, i).start()

                @pl.when(g > 0)
                def _():
                    for j in range(2):
                        csum[s, f, i, 2 * g + j] = total[j * half : (j + 1) * half].astype(jnp.bfloat16)

                    @pl.when(is_self(s))
                    def _():
                        for j in range(2):
                            obuf[y, f, i, 2 * g + j] = csum[s, f, i, 2 * g + j]

                    @pl.when(jnp.logical_not(is_self(s)))
                    def _():
                        out(g, s, f, i).start()

                return carry

            lax.fori_loop(0, 4, one, 0)

    wz(0).start()
    for copy in inputs:
        copy.wait()

    def attend_loop(k, carry):
        attend_rank(k)

        @pl.when(k % 2 == 1)
        def _():
            finish_group(k // 2)

        @pl.when(k == 1)
        def _():
            for p in range(AHEAD):
                send_rows(p)
            for i in range(2):
                local_w(i).wait()
                twin(own, i).start()

        @pl.when(k >= 3)
        def _():
            pass_on(k - 3)

        return carry

    lax.fori_loop(0, slots, attend_loop, 0)

    def pass_loop(p, carry):
        pass_on(p)
        return carry

    def step(u, carry):
        @pl.when(u == 0)
        def _():
            for i in range(2):
                twin_in(own, i).wait_recv()
            pass_on(3)
            wz(0).wait_send()
            wz(1).start()
            forwarded(0)

        @pl.when(u == 2)
        def _():
            lax.fori_loop(4, PIECES, pass_loop, 0)
            wz_in(0).wait_recv()
            twin(oth, 0).start()
            forwarded(1)

        @pl.when(u == 4)
        def _():
            twin_in(oth, 0).wait_recv()

        @pl.when(u == 6)
        def _():
            wz_in(1).wait_recv()
            twin(oth, 1).start()
            twin_in(oth, 1).wait_recv()

        @pl.when(u == 8)
        def _():
            forwarded(2)

        compute(u)

        @pl.when(u >= LAG)
        def _():
            reduce(u - LAG)

        return carry

    lax.fori_loop(0, UNITS, step, 0)
    for u in range(UNITS - LAG, UNITS):
        reduce(u)

    wz(1).wait_send()
    for i in range(2):
        twin(own, i).wait_send()
        twin(oth, i).wait_send()

    def passed(p, carry):
        @pl.when(p >= PIECES - AHEAD)
        def _():
            rows_left(p)

        forward(p, oth).wait_send()

        @pl.when(inner)
        def _():
            forward(p, own).wait_send()

        return carry

    lax.fori_loop(0, PIECES, passed, 0)

    def sent(u, carry):
        g, f, i = unit(u)

        @pl.when(jnp.logical_not(keeper))
        def _():
            x_copy(g, f, i).wait_send()

        @pl.when(keeper)
        def _():
            def gone(s, carry):
                @pl.when(g == 0)
                def _():
                    for j in range(2):
                        out0(j, s, f, i).wait_send()

                @pl.when(jnp.logical_and(g > 0, jnp.logical_not(is_self(s))))
                def _():
                    out(g, s, f, i).wait_send()

                return carry

            lax.fori_loop(0, 4, gone, 0)

        return carry

    lax.fori_loop(0, UNITS, sent, 0)

    def columns(f, yy, i, cc):
        first = f * 4 * wide + yy * 2 * wide + cc * wide + i * wrows
        return slice(first, first + wrows)

    for f in range(2):
        for i in range(2):
            for yy in range(2):
                for j in range(2):
                    remote(
                        csum.at[0, 0, 0, 0], obuf.at[yy, f, i, j], o_send0.at[0, 0, 0, 0],
                        o_recv0.at[j, yy, f, i], at(z, y, 1 - c, x),
                    ).wait_recv()
                for g in range(1, GROUPS):
                    @pl.when(jnp.logical_not(jnp.logical_and(jnp.logical_and(keeper, outer), y == yy)))
                    def _():
                        remote(
                            csum.at[0, 0, 0, pl.ds(0, 2)], obuf.at[yy, f, i, pl.ds(2 * g, 2)], o_send.at[0, 0, 0, 0],
                            o_recv.at[g - 1, yy, f, i], at(z, y, 1 - c, x),
                        ).wait_recv()

    for slot in range(slots):
        rank = order_ref[slots + slot]
        for f in range(2):
            for i in range(2):
                for yy in range(2):
                    for cc in range(2):
                        o_ref[slot, :, columns(f, yy, i, cc)] = obuf[
                            yy, f, i, rank, :, cc * wrows : (cc + 1) * wrows
                        ]


def fused(queries, fresh_kv, pages, lengths, table, movers, w_out):
    slots, tokens, width = queries.shape
    wide = w_out.shape[0]
    kv_heads = fresh_kv.shape[2] // (2 * HEAD_SIZE)
    qrows = width // (kv_heads * HEAD_SIZE) * tokens
    rows = slots * tokens // GROUPS
    pool, page, maxp = pages.shape[0], pages.shape[1], table.shape[1]
    most = [-(-MOVER_POSITIONS // page)] * 2
    for i in range(slots - 2):
        most.append(min(maxp, (pool - 2 - i) // (slots - 2 - i)))
    rank_steps = tuple(-(-m // STEP_PAGES) for m in most)
    dma = pltpu.SemaphoreType.DMA
    smem, hbm = pl.BlockSpec(memory_space=pltpu.SMEM), pl.BlockSpec(memory_space=pl.ANY)
    b, f32 = jnp.bfloat16, jnp.float32
    done = pl.pallas_call(
        functools.partial(fused_kernel, rank_steps),
        out_shape=jax.ShapeDtypeStruct((slots, tokens, 8 * wide), b),
        in_specs=[hbm, hbm, hbm, smem, smem, smem, hbm],
        out_specs=pl.BlockSpec(memory_space=pltpu.VMEM),
        scratch_shapes=[
            pltpu.VMEM(queries.shape, b),
            pltpu.VMEM(fresh_kv.shape, b),
            pltpu.VMEM(pages.shape, b),
            pltpu.SMEM((2 * slots,), jnp.int32),
            pltpu.VMEM((kv_heads, qrows, HEAD_SIZE), b),
            pltpu.VMEM((kv_heads, qrows, 1), f32),
            pltpu.VMEM((2, kv_heads, qrows, 1), f32),
            pltpu.VMEM((2, kv_heads, qrows, HEAD_SIZE), f32),
            pltpu.VMEM((GROUPS, rows, width), b),
            pltpu.VMEM((GROUPS, 4, rows, width), b),
            pltpu.VMEM((2, 2, 2, wide // 2, width), b),
            pltpu.VMEM((GROUPS, 2, 2, 4 * rows, wide), b),
            pltpu.VMEM((GROUPS, 2, 2, 4 * rows, wide), b),
            pltpu.VMEM((GROUPS, 2, 2, 4 * rows, wide), f32),
            pltpu.VMEM((4, 2, 2, slots, tokens, wide), b),
            pltpu.VMEM((2, 2, 2, slots, tokens, wide), b),
            dma((3,)), dma((2,)), dma((2,)), dma((2,)), dma((2, 2)), dma((2, 2)),
            dma((PIECES,)), dma((PIECES,)), dma((PIECES, 2)), dma((PIECES, 2)), dma((PIECES, 2)),
            dma((GROUPS, 2, 2)), dma((GROUPS, 2, 2)),
            dma((2, 4, 2, 2)), dma((GROUPS - 1, 4, 2, 2)), dma((2, 2, 2, 2)), dma((GROUPS - 1, 2, 2, 2)),
        ],
        compiler_params=pltpu.CompilerParams(
            collective_id=0, has_side_effects=True, vmem_limit_bytes=56 << 20
        ),
    )(queries, fresh_kv, pages, lengths, table, movers, w_out)
    return done.reshape(slots * tokens, 8 * wide)


def per_device(queries, fresh_kv, key_value_pages, cache_lengths, page_table, movers, w_out):
    slots, tokens, width = queries.shape
    to_next = movers[0, 0]
    to_prev = movers[0, 1]
    if lax.axis_size("tp") == 2 and lax.axis_size("req") == 16 and slots == 2 * GROUPS:
        return fused(queries, fresh_kv, key_value_pages, cache_lengths, page_table, movers, w_out)
    attended = attend(queries, fresh_kv, key_value_pages, cache_lengths, page_table)
    from_left = passed_along(attended[to_next], "req", 1)
    from_right = passed_along(attended[to_prev], "req", -1)
    slot_ids = jnp.arange(slots, dtype=jnp.int32)[:, None, None]
    placed = jnp.where(
        slot_ids == to_next, from_left[None], jnp.where(slot_ids == to_prev, from_right[None], attended)
    )
    flat = placed.reshape(slots * tokens, width)
    partial_sum = lax.dot_general(
        flat,
        lax.all_gather(w_out, "req", axis=0, tiled=True),
        (((1,), (1,)), ((), ())),
        preferred_element_type=jnp.float32,
    )
    return lax.psum_scatter(partial_sum, "tp", scatter_dimension=1, tiled=True).astype(jnp.bfloat16)


def solution(mesh):
    return jax.shard_map(
        per_device,
        mesh=mesh,
        in_specs=(
            P("req", None, "tp"),
            P("req", None, "tp"),
            P("req", None, "tp"),
            P("req"),
            P("req", None),
            P("req", None),
            P("req", "tp"),
        ),
        out_specs=P("req", "tp"),
        check_vma=False,
    )
```

```python
import functools

import jax
import jax.numpy as jnp
from jax import lax
from jax.experimental import pallas as pl
from jax.experimental.pallas import tpu as pltpu
from jax.sharding import PartitionSpec as P

HEAD_SIZE = 128
PAGE_GROUP = 8
LOG2E = 1.4426950408889634
MASKED = -1e30


def passed_along(block, axis, distance):
    devices = range(lax.axis_size(axis))
    route = [((i - distance) % len(devices), i) for i in devices]
    return lax.ppermute(block, axis, route)


def nt(a, b):
    return lax.dot_general(a, b, (((1,), (1,)), ((), ())), preferred_element_type=jnp.float32)


def attend_kernel(kv_heads, group, len_ref, tab_ref, q_ref, f_ref, pages_ref, o_ref, qs, ms, ls, acc):
    slot = pl.program_id(0)
    tokens = q_ref.shape[1]
    page = pages_ref.shape[1]
    rows = group * tokens
    maxp = tab_ref.shape[1]
    length = len_ref[slot]
    factor = HEAD_SIZE ** (-0.5) * LOG2E
    span = PAGE_GROUP * page
    groups = (length + span - 1) // span
    token = lax.broadcasted_iota(jnp.int32, (rows, tokens), 0) % tokens
    newer = lax.broadcasted_iota(jnp.int32, (rows, tokens), 1)
    for g in range(kv_heads):
        heads = [
            q_ref[0, :, (g * group + h) * HEAD_SIZE : (g * group + h + 1) * HEAD_SIZE].astype(jnp.float32)
            for h in range(group)
        ]
        q = jnp.concatenate(heads, axis=0).astype(jnp.bfloat16)
        qs[g] = q
        key = f_ref[0, :, 2 * g * HEAD_SIZE : (2 * g + 1) * HEAD_SIZE]
        value = f_ref[0, :, (2 * g + 1) * HEAD_SIZE : (2 * g + 2) * HEAD_SIZE]
        s = jnp.where(newer <= token, nt(q, key), MASKED)
        m = jnp.max(s, axis=-1, keepdims=True)
        p = jnp.exp2((s - m) * factor)
        ms[g] = m
        ls[g] = jnp.sum(p, axis=-1, keepdims=True)
        acc[g] = jnp.dot(p.astype(jnp.bfloat16), value, preferred_element_type=jnp.float32)

    def body(at, carry):
        ids = [tab_ref[slot, jnp.minimum(at * PAGE_GROUP + u, maxp - 1)] for u in range(PAGE_GROUP)]
        pos = at * span + lax.broadcasted_iota(jnp.int32, (rows, span), 1)
        valid = pos < length
        def side(g, which):
            first = (2 * g + which) * HEAD_SIZE
            return jnp.concatenate([pages_ref[i, :, first : first + HEAD_SIZE] for i in ids], axis=0)

        def scored(g):
            return jnp.where(valid, nt(qs[g], side(g, 0)), MASKED)

        s = scored(0)
        for g in range(kv_heads):
            following = scored(g + 1) if g + 1 < kv_heads else None
            before = ms[g]
            m = jnp.maximum(before, jnp.max(s, axis=-1, keepdims=True))
            fade = jnp.exp2((before - m) * factor)
            p = jnp.exp2((s - m) * factor)
            ms[g] = m
            ls[g] = ls[g] * fade + jnp.sum(p, axis=-1, keepdims=True)
            acc[g] = acc[g] * fade + jnp.dot(
                p.astype(jnp.bfloat16), side(g, 1), preferred_element_type=jnp.float32
            )
            s = following
        return carry

    lax.fori_loop(0, groups, body, 0)
    for g in range(kv_heads):
        o = acc[g] / ls[g]
        for h in range(group):
            o_ref[0, :, (g * group + h) * HEAD_SIZE : (g * group + h + 1) * HEAD_SIZE] = o[
                h * tokens : (h + 1) * tokens
            ].astype(jnp.bfloat16)


def attend(queries, fresh_kv, pages, lengths, table):
    slots, tokens, width = queries.shape
    kv_heads = fresh_kv.shape[2] // (2 * HEAD_SIZE)
    group = width // (kv_heads * HEAD_SIZE)
    rows = group * tokens
    return pl.pallas_call(
        functools.partial(attend_kernel, kv_heads, group),
        out_shape=jax.ShapeDtypeStruct(queries.shape, jnp.bfloat16),
        grid_spec=pltpu.PrefetchScalarGridSpec(
            num_scalar_prefetch=2,
            grid=(slots,),
            in_specs=[
                pl.BlockSpec((1, tokens, width), lambda s, a, b: (s, 0, 0)),
                pl.BlockSpec((1, tokens, fresh_kv.shape[2]), lambda s, a, b: (s, 0, 0)),
                pl.BlockSpec(pages.shape, lambda s, a, b: (0, 0, 0), pipeline_mode=pl.Buffered(1)),
            ],
            out_specs=pl.BlockSpec((1, tokens, width), lambda s, a, b: (s, 0, 0)),
            scratch_shapes=[
                pltpu.VMEM((kv_heads, rows, HEAD_SIZE), jnp.bfloat16),
                pltpu.VMEM((kv_heads, rows, 1), jnp.float32),
                pltpu.VMEM((kv_heads, rows, 1), jnp.float32),
                pltpu.VMEM((kv_heads, rows, HEAD_SIZE), jnp.float32),
            ],
        ),
        compiler_params=pltpu.CompilerParams(vmem_limit_bytes=40 << 20),
        cost_estimate=pl.CostEstimate(
            flops=4 * rows * kv_heads * pages.shape[0] * pages.shape[1] * HEAD_SIZE,
            transcendentals=rows * kv_heads * pages.shape[0] * pages.shape[1],
            bytes_accessed=pages.size * 2 + queries.size * 4,
        ),
    )(lengths, table, queries, fresh_kv, pages)

MESH = pl.DeviceIdType.MESH
GROUPS = 3
PARTS = 4
PIECES = GROUPS * PARTS
AHEAD = 3
WPARTS = 16
WFIRST = 4
WPER = (WPARTS - WFIRST) // PIECES
UNITS = 12
LAG = 2
STEP_PAGES = 4
MOVER_POSITIONS = 512
UNIT_G = (0, 0, 1, 1, 0, 1, 2, 2, 2, 0, 1, 2)
UNIT_F = (0, 0, 0, 0, 1, 1, 0, 0, 1, 1, 1, 1)
UNIT_I = (0, 1, 0, 1, 0, 0, 0, 1, 0, 1, 1, 1)
PASS_AT = (14, 19, 25, 32, 39, 45)


def pick(at, table):
    value = table[0]
    for k in range(1, len(table)):
        if table[k] != table[k - 1]:
            value = jnp.where(at >= k, table[k], value)
    return value


def fused_kernel(
    rank_steps,
    q_any, f_any, pages_any, len_ref, tab_ref, mov_ref, w_ref, o_ref,
    q_ref, f_ref, pages_ref, order_ref, qs, scores, ms, ls, sums, acc, att_ref,
    abuf, wbuf, psend, precv, ploc, csum, obuf,
    in_sem, wl_sem, wz_send, wz_recv, wt_send, wt_recv, a1_send, a2_send, f_send, az_recv, ay_recv,
    x_send, x_recv, o_send0, o_send, o_recv0, o_recv,
):
    me, x = lax.axis_index("req"), lax.axis_index("tp")
    n = 16
    z, y, c = me // 4, (me // 2) % 2, me % 2
    own = z % 2
    oth = 1 - own
    t = z // 2
    inner = jnp.logical_or(z == 1, z == 2)
    outer = jnp.logical_not(inner)
    far = 2 - t
    zp = z + 1 - 2 * own
    keeper = x == t
    mine = 2 * y + own
    kept = jnp.where(keeper, 1 - y, y)
    rows = att_ref.shape[1]
    slots, tokens = q_ref.shape[0], q_ref.shape[1]
    kv_heads, group = qs.shape[0], qs.shape[1] // q_ref.shape[1]
    page = pages_ref.shape[1]
    maxp = tab_ref.shape[1]
    qrows = group * tokens
    factor = HEAD_SIZE ** (-0.5) * LOG2E
    wide = w_ref.shape[0]
    wrows = wide // 2
    cols = att_ref.shape[2] // PARTS

    def at(zz, yy, cc, xx):
        return {"req": zz * 4 + yy * 2 + cc, "tp": xx}

    def remote(src, dst, ss, rs, dev):
        return pltpu.make_async_remote_copy(
            src_ref=src, dst_ref=dst, send_sem=ss, recv_sem=rs, device_id=dev, device_id_type=MESH
        )

    barrier = pltpu.get_barrier_semaphore()
    my_index = me * 2 + x

    def greet(i, carry):
        target = (my_index + i) % (2 * n)
        pl.semaphore_signal(
            barrier, inc=1, device_id={"req": target // 2, "tp": target % 2}, device_id_type=MESH
        )
        return carry

    lax.fori_loop(1, 2 * n, greet, 0)

    def local_w(i):
        return pltpu.make_async_copy(w_ref.at[pl.ds(i * wrows, wrows)], wbuf.at[own, i, c], wl_sem.at[i])

    inputs = [
        pltpu.make_async_copy(q_any, q_ref, in_sem.at[0]),
        pltpu.make_async_copy(f_any, f_ref, in_sem.at[1]),
        pltpu.make_async_copy(pages_any, pages_ref, in_sem.at[2]),
    ]
    for copy in inputs:
        copy.start()
    for i in range(2):
        local_w(i).start()

    keys = []
    for slot in range(slots):
        key = len_ref[slot] * slots + slot
        key = jnp.where(mov_ref[0, 1] == slot, -1, key)
        keys.append(jnp.where(mov_ref[0, 0] == slot, -2, key))
    ranks = []
    for slot in range(slots):
        rank = 0
        for i in range(slots):
            if i != slot:
                rank = rank + jnp.where(keys[i] < keys[slot], 1, 0)
        ranks.append(rank)
    for k in range(slots):
        slot_at = 0
        for slot in range(1, slots):
            slot_at = slot_at + jnp.where(ranks[slot] == k, slot, 0)
        order_ref[k] = slot_at
        order_ref[slots + k] = ranks[k]
    pl.semaphore_wait(barrier, 2 * n - 1)

    wpart = wide // WPARTS
    whalf = WPARTS // 2

    def wz(k):
        part = pl.ds(pl.multiple_of(k * wpart, wpart), wpart)
        there = pl.ds(pl.multiple_of(k % whalf * wpart, wpart), wpart)
        return remote(
            w_ref.at[part], wbuf.at[own, k // whalf, c, there], wz_send.at[k], wz_recv.at[k], at(zp, y, c, x)
        )

    def wz_in(k):
        where = wbuf.at[oth, k // whalf, c, pl.ds(pl.multiple_of(k % whalf * wpart, wpart), wpart)]
        return remote(where, where, wz_send.at[k], wz_recv.at[k], at(zp, y, c, x))

    def w_half(i):
        def one(k, carry):
            wz_in(k).wait_recv()
            return carry

        lax.fori_loop(i * whalf, (i + 1) * whalf, one, 0)
        twin(oth, i).start()

    def twin(f, i):
        src = w_ref.at[pl.ds(i * wrows, wrows)] if f is own else wbuf.at[f, i, c]
        return remote(src, wbuf.at[f, i, c], wt_send.at[f, i], wt_recv.at[f, i], at(z, y, 1 - c, x))

    def twin_in(f, i):
        where = wbuf.at[f, i, 1 - c]
        return remote(where, where, wt_send.at[f, i], wt_recv.at[f, i], at(z, y, 1 - c, x))

    token = lax.broadcasted_iota(jnp.int32, (qrows, tokens), 0) % tokens
    newer = lax.broadcasted_iota(jnp.int32, (qrows, tokens), 1)
    span = STEP_PAGES * page

    lanes = (qrows, HEAD_SIZE)

    def fresh_scores(slot, g):
        key = f_ref[slot, :, 2 * g * HEAD_SIZE : (2 * g + 1) * HEAD_SIZE]
        return jnp.where(newer <= token, nt(qs[g], key), MASKED)

    def tiles(a):
        return [a[:, i * HEAD_SIZE : (i + 1) * HEAD_SIZE] for i in range(a.shape[1] // HEAD_SIZE)]

    def attend_start(slot):
        for g in range(kv_heads):
            heads = [
                q_ref[slot, :, (g * group + h) * HEAD_SIZE : (g * group + h + 1) * HEAD_SIZE].astype(jnp.float32)
                for h in range(group)
            ]
            qs[g] = jnp.concatenate(heads, axis=0).astype(jnp.bfloat16)
            ms[g] = jnp.broadcast_to(jnp.max(fresh_scores(slot, g), axis=-1, keepdims=True), lanes)

    def page_side(slot, at_step, g, which):
        first = (2 * g + which) * HEAD_SIZE
        ids = [tab_ref[slot, jnp.minimum(at_step * STEP_PAGES + u, maxp - 1)] for u in range(STEP_PAGES)]
        return jnp.concatenate([pages_ref[i, :, first : first + HEAD_SIZE] for i in ids], axis=0)

    def score_step(slot, at_step):
        pos = at_step * span + lax.broadcasted_iota(jnp.int32, (1, span), 1)
        bias = jnp.where(pos < len_ref[slot], 0.0, MASKED)
        for g in range(kv_heads):
            s = nt(qs[g], page_side(slot, at_step, g, 0)) + bias
            scores[at_step, g] = s
            ms[g] = functools.reduce(jnp.maximum, tiles(s), ms[g])

    def attend_middle(slot, j):
        for g in range(kv_heads):
            m = jnp.max(ms[g], axis=-1, keepdims=True)
            p = jnp.exp2((fresh_scores(slot, g) - m) * factor)
            value = f_ref[slot, :, (2 * g + 1) * HEAD_SIZE : (2 * g + 2) * HEAD_SIZE]
            ms[g] = jnp.broadcast_to(m, lanes)
            ls[j, g] = jnp.sum(p, axis=-1, keepdims=True)
            sums[j, g] = jnp.zeros(lanes, jnp.float32)
            acc[j, g] = jnp.dot(p.astype(jnp.bfloat16), value, preferred_element_type=jnp.float32)

    def value_step(slot, j, at_step):
        for g in range(kv_heads):
            m = ms[g]
            p = [jnp.exp2((a - m) * factor) for a in tiles(scores[at_step, g])]
            sums[j, g] += functools.reduce(jnp.add, p)
            weights = jnp.concatenate(p, axis=1).astype(jnp.bfloat16)
            acc[j, g] += jnp.dot(weights, page_side(slot, at_step, g, 1), preferred_element_type=jnp.float32)

    def finish_group(at_group):
        for g in range(kv_heads):
            o = [acc[j, g] / (ls[j, g] + jnp.sum(sums[j, g], axis=-1, keepdims=True)) for j in range(2)]
            for h in range(group):
                lane = (g * group + h) * HEAD_SIZE
                att_ref[at_group, :, lane : lane + HEAD_SIZE] = jnp.concatenate(
                    [o[j][h * tokens : (h + 1) * tokens] for j in range(2)], axis=0
                ).astype(jnp.bfloat16)

        @pl.when(outer)
        def _():
            abuf[at_group, mine] = att_ref[at_group]

    def rows_of(p):
        return att_ref.at[p // PARTS, :, pl.ds(pl.multiple_of((p % PARTS) * cols, cols), cols)]

    def place(p, s):
        return abuf.at[p // PARTS, s, :, pl.ds(pl.multiple_of((p % PARTS) * cols, cols), cols)]

    def a1_outer(p):
        return remote(rows_of(p), place(p, mine), a1_send.at[p], ay_recv.at[p, own], at(z, 1 - y, c, x))

    def a1_inner(p):
        return remote(rows_of(p), place(p, mine), a1_send.at[p], az_recv.at[p, own], at(zp, y, c, x))

    def a2(p):
        return remote(rows_of(p), place(p, mine), a2_send.at[p], az_recv.at[p, own], at(far, y, c, x))

    def z_in(p, q):
        where = place(p, 2 * y + q)
        return remote(where, where, a1_send.at[p], az_recv.at[p, q], at(zp, y, c, x))

    def forward(p, q):
        where = place(p, 2 * y + q)
        return remote(where, where, f_send.at[p, q], ay_recv.at[p, q], at(z, 1 - y, c, x))

    def y_in(p, q):
        where = place(p, 2 * (1 - y) + q)
        return remote(where, where, f_send.at[p, q], ay_recv.at[p, q], at(z, 1 - y, c, x))

    def send_rows(p):
        a2(p).start()

        @pl.when(inner)
        def _():
            a1_inner(p).start()

        @pl.when(outer)
        def _():
            a1_outer(p).start()

    def rows_left(p):
        a2(p).wait_send()
        a1_inner(p).wait_send()

    def pass_on(p):
        z_in(p, oth).wait_recv()
        forward(p, oth).start()

        @pl.when(inner)
        def _():
            z_in(p, own).wait_recv()
            forward(p, own).start()

        @pl.when(p < PIECES - AHEAD)
        def _():
            rows_left(p)
            send_rows(p + AHEAD)

        for k in range(WPER):
            wz(WFIRST + p * WPER + k).start()

    def forwarded(g):
        def one(h, carry):
            for q in range(2):
                y_in(g * PARTS + h, q).wait_recv()
            return carry

        lax.fori_loop(0, PARTS, one, 0)

    def unit(u):
        f = pick(u, UNIT_F)
        return pick(u, UNIT_G), jnp.where(f == 0, own, oth), pick(u, UNIT_I)

    def x_copy(g, f, i):
        return remote(
            psend.at[g, f, i], precv.at[g, f, i], x_send.at[g, f, i], x_recv.at[g, f, i], at(z, y, c, 1 - x)
        )

    def compute(u):
        g, f, i = unit(u)
        a = abuf[g].reshape(4 * rows, abuf.shape[3])
        part = nt(a, wbuf[f, i].reshape(2 * wrows, wbuf.shape[4]))

        low, high = part[: 2 * rows], part[2 * rows :]
        first = kept == 0
        ploc[g, f, i] = jnp.where(first, low, high)
        psend[g, f, i] = jnp.where(first, high, low).astype(jnp.bfloat16)
        x_copy(g, f, i).start()

    def out0(j, q, f, i):
        r = (2 * own + q) * 4 + kept * 2 + c
        dest = (r + n + 1 - 2 * j) % n
        return remote(
            csum.at[q, f, i, j], obuf.at[y, f, i, j], o_send0.at[j, q, f, i], o_recv0.at[j, y, f, i],
            {"req": dest, "tp": t},
        )

    def out(g, q, f, i):
        pair = pl.ds(2 * g, 2)
        return remote(
            csum.at[q, f, i, pair], obuf.at[y, f, i, pair], o_send.at[g - 1, q, f, i],
            o_recv.at[g - 1, y, f, i], at(2 * own + q, kept, c, t),
        )

    half = rows // 2

    def reduce(u):
        g, f, i = unit(u)
        x_copy(g, f, i).wait_recv()
        for q in range(2):
            total = ploc[g, f, i, q * rows : (q + 1) * rows] + precv[g, f, i, q * rows : (q + 1) * rows].astype(
                jnp.float32
            )
            for j in range(2):
                csum[q, f, i, 2 * g + j] = total[j * half : (j + 1) * half].astype(jnp.bfloat16)

        @pl.when(g == 0)
        def _():
            for q in range(2):
                for j in range(2):
                    out0(j, q, f, i).start()

        @pl.when(g > 0)
        def _():
            for q in range(2):
                out(g, q, f, i).start()

    for k in range(WFIRST):
        wz(k).start()
    for copy in inputs:
        copy.wait()

    ranks_at, starts, ends, tops = [], [], [], []
    for k, steps in enumerate(rank_steps):
        starts += [len(ranks_at)] * 2 * steps
        tops += [steps] * 2 * steps
        ranks_at += [k] * 2 * steps
        ends.append(len(ranks_at) - 1)

    def attend_loop(tick, carry):
        k = pick(tick, ranks_at)
        top = pick(tick, tops)
        in_rank = tick - pick(tick, starts)
        slot = order_ref[k]
        j = k % 2

        @pl.when(in_rank == 0)
        def _():
            attend_start(slot)

        @pl.when(in_rank < top)
        def _():
            score_step(slot, in_rank)

        @pl.when(in_rank == top)
        def _():
            attend_middle(slot, j)

        @pl.when(in_rank >= top)
        def _():
            value_step(slot, j, in_rank - top)

        @pl.when(functools.reduce(jnp.logical_or, [tick == e for e in ends[1::2]]))
        def _():
            finish_group(k // 2)

        @pl.when(tick == ends[1])
        def _():
            for p in range(AHEAD):
                send_rows(p)
            for i in range(2):
                local_w(i).wait()
                twin(own, i).start()

        for p, when in enumerate(PASS_AT):
            @pl.when(tick == when)
            def _():
                pass_on(p)

        return carry

    lax.fori_loop(0, len(ranks_at), attend_loop, 0)

    def pass_loop(p, carry):
        pass_on(p)
        return carry

    def step(u, carry):
        @pl.when(u == 0)
        def _():
            for i in range(2):
                twin_in(own, i).wait_recv()
            forwarded(0)

        @pl.when(u == 2)
        def _():
            lax.fori_loop(len(PASS_AT), PIECES - 2, pass_loop, 0)
            forwarded(1)

        @pl.when(u == 4)
        def _():
            w_half(0)
            twin_in(oth, 0).wait_recv()

        @pl.when(u == 6)
        def _():
            lax.fori_loop(PIECES - 2, PIECES, pass_loop, 0)
            forwarded(2)

        @pl.when(u == 9)
        def _():
            w_half(1)
            twin_in(oth, 1).wait_recv()

        compute(u)

        @pl.when(u >= LAG)
        def _():
            reduce(u - LAG)

        return carry

    lax.fori_loop(0, UNITS, step, 0)
    for u in range(UNITS - LAG, UNITS):
        reduce(u)

    def weights_left(k, carry):
        wz(k).wait_send()
        return carry

    lax.fori_loop(0, WPARTS, weights_left, 0)
    for i in range(2):
        twin(own, i).wait_send()
        twin(oth, i).wait_send()

    def passed(p, carry):
        @pl.when(p >= PIECES - AHEAD)
        def _():
            rows_left(p)

        forward(p, oth).wait_send()

        @pl.when(inner)
        def _():
            forward(p, own).wait_send()

        return carry

    lax.fori_loop(0, PIECES, passed, 0)

    def sent(u, carry):
        g, f, i = unit(u)

        x_copy(g, f, i).wait_send()

        @pl.when(g == 0)
        def _():
            for q in range(2):
                for j in range(2):
                    out0(j, q, f, i).wait_send()

        @pl.when(g > 0)
        def _():
            for q in range(2):
                out(g, q, f, i).wait_send()

        return carry

    lax.fori_loop(0, UNITS, sent, 0)

    def columns(f, yy, i, cc):
        first = f * 4 * wide + yy * 2 * wide + cc * wide + i * wrows
        return slice(first, first + wrows)

    for f in range(2):
        for i in range(2):
            for yy in range(2):
                for j in range(2):
                    remote(
                        csum.at[0, 0, 0, 0], obuf.at[yy, f, i, j], o_send0.at[0, 0, 0, 0],
                        o_recv0.at[j, yy, f, i], at(z, y, 1 - c, x),
                    ).wait_recv()
                for g in range(1, GROUPS):
                    remote(
                        csum.at[0, 0, 0, pl.ds(0, 2)], obuf.at[yy, f, i, pl.ds(2 * g, 2)], o_send.at[0, 0, 0, 0],
                        o_recv.at[g - 1, yy, f, i], at(z, y, 1 - c, x),
                    ).wait_recv()

    for slot in range(slots):
        rank = order_ref[slots + slot]
        for f in range(2):
            for i in range(2):
                for yy in range(2):
                    for cc in range(2):
                        o_ref[slot, :, columns(f, yy, i, cc)] = obuf[
                            yy, f, i, rank, :, cc * wrows : (cc + 1) * wrows
                        ]


def fused(queries, fresh_kv, pages, lengths, table, movers, w_out):
    slots, tokens, width = queries.shape
    wide = w_out.shape[0]
    kv_heads = fresh_kv.shape[2] // (2 * HEAD_SIZE)
    qrows = width // (kv_heads * HEAD_SIZE) * tokens
    rows = slots * tokens // GROUPS
    pool, page, maxp = pages.shape[0], pages.shape[1], table.shape[1]
    most = [-(-MOVER_POSITIONS // page)] * 2
    for i in range(slots - 2):
        most.append(min(maxp, (pool - 2 - i) // (slots - 2 - i)))
    rank_steps = tuple(-(-m // STEP_PAGES) for m in most)
    dma = pltpu.SemaphoreType.DMA
    smem, hbm = pl.BlockSpec(memory_space=pltpu.SMEM), pl.BlockSpec(memory_space=pl.ANY)
    b, f32 = jnp.bfloat16, jnp.float32
    done = pl.pallas_call(
        functools.partial(fused_kernel, rank_steps),
        out_shape=jax.ShapeDtypeStruct((slots, tokens, 8 * wide), b),
        in_specs=[hbm, hbm, hbm, smem, smem, smem, hbm],
        out_specs=pl.BlockSpec(memory_space=pltpu.VMEM),
        scratch_shapes=[
            pltpu.VMEM(queries.shape, b),
            pltpu.VMEM(fresh_kv.shape, b),
            pltpu.VMEM(pages.shape, b),
            pltpu.SMEM((2 * slots,), jnp.int32),
            pltpu.VMEM((kv_heads, qrows, HEAD_SIZE), b),
            pltpu.VMEM((max(rank_steps), kv_heads, qrows, STEP_PAGES * page), f32),
            pltpu.VMEM((kv_heads, qrows, HEAD_SIZE), f32),
            pltpu.VMEM((2, kv_heads, qrows, 1), f32),
            pltpu.VMEM((2, kv_heads, qrows, HEAD_SIZE), f32),
            pltpu.VMEM((2, kv_heads, qrows, HEAD_SIZE), f32),
            pltpu.VMEM((GROUPS, rows, width), b),
            pltpu.VMEM((GROUPS, 4, rows, width), b),
            pltpu.VMEM((2, 2, 2, wide // 2, width), b),
            pltpu.VMEM((GROUPS, 2, 2, 2 * rows, wide), b),
            pltpu.VMEM((GROUPS, 2, 2, 2 * rows, wide), b),
            pltpu.VMEM((GROUPS, 2, 2, 2 * rows, wide), f32),
            pltpu.VMEM((2, 2, 2, slots, tokens, wide), b),
            pltpu.VMEM((2, 2, 2, slots, tokens, wide), b),
            dma((3,)), dma((2,)), dma((WPARTS,)), dma((WPARTS,)), dma((2, 2)), dma((2, 2)),
            dma((PIECES,)), dma((PIECES,)), dma((PIECES, 2)), dma((PIECES, 2)), dma((PIECES, 2)),
            dma((GROUPS, 2, 2)), dma((GROUPS, 2, 2)),
            dma((2, 2, 2, 2)), dma((GROUPS - 1, 2, 2, 2)), dma((2, 2, 2, 2)), dma((GROUPS - 1, 2, 2, 2)),
        ],
        compiler_params=pltpu.CompilerParams(
            collective_id=0, has_side_effects=True, vmem_limit_bytes=60 << 20
        ),
    )(queries, fresh_kv, pages, lengths, table, movers, w_out)
    return done.reshape(slots * tokens, 8 * wide)


def per_device(queries, fresh_kv, key_value_pages, cache_lengths, page_table, movers, w_out):
    slots, tokens, width = queries.shape
    to_next = movers[0, 0]
    to_prev = movers[0, 1]
    if lax.axis_size("tp") == 2 and lax.axis_size("req") == 16 and slots == 2 * GROUPS:
        return fused(queries, fresh_kv, key_value_pages, cache_lengths, page_table, movers, w_out)
    attended = attend(queries, fresh_kv, key_value_pages, cache_lengths, page_table)
    from_left = passed_along(attended[to_next], "req", 1)
    from_right = passed_along(attended[to_prev], "req", -1)
    slot_ids = jnp.arange(slots, dtype=jnp.int32)[:, None, None]
    placed = jnp.where(
        slot_ids == to_next, from_left[None], jnp.where(slot_ids == to_prev, from_right[None], attended)
    )
    flat = placed.reshape(slots * tokens, width)
    partial_sum = lax.dot_general(
        flat,
        lax.all_gather(w_out, "req", axis=0, tiled=True),
        (((1,), (1,)), ((), ())),
        preferred_element_type=jnp.float32,
    )
    return lax.psum_scatter(partial_sum, "tp", scatter_dimension=1, tiled=True).astype(jnp.bfloat16)


def solution(mesh):
    return jax.shard_map(
        per_device,
        mesh=mesh,
        in_specs=(
            P("req", None, "tp"),
            P("req", None, "tp"),
            P("req", None, "tp"),
            P("req"),
            P("req", None),
            P("req", None),
            P("req", "tp"),
        ),
        out_specs=P("req", "tp"),
        check_vma=False,
    )
```

```python
import functools

import jax
import jax.numpy as jnp
from jax import lax
from jax.experimental import pallas as pl
from jax.experimental.pallas import tpu as pltpu
from jax.sharding import PartitionSpec as P

HEAD_SIZE = 128
PAGE_GROUP = 8
LOG2E = 1.4426950408889634
MASKED = -1e30


def passed_along(block, axis, distance):
    devices = range(lax.axis_size(axis))
    route = [((i - distance) % len(devices), i) for i in devices]
    return lax.ppermute(block, axis, route)


def nt(a, b):
    return lax.dot_general(a, b, (((1,), (1,)), ((), ())), preferred_element_type=jnp.float32)


def attend_kernel(kv_heads, group, len_ref, tab_ref, q_ref, f_ref, pages_ref, o_ref, qs, ms, ls, acc):
    slot = pl.program_id(0)
    tokens = q_ref.shape[1]
    page = pages_ref.shape[1]
    rows = group * tokens
    maxp = tab_ref.shape[1]
    length = len_ref[slot]
    factor = HEAD_SIZE ** (-0.5) * LOG2E
    span = PAGE_GROUP * page
    groups = (length + span - 1) // span
    token = lax.broadcasted_iota(jnp.int32, (rows, tokens), 0) % tokens
    newer = lax.broadcasted_iota(jnp.int32, (rows, tokens), 1)
    for g in range(kv_heads):
        heads = [
            q_ref[0, :, (g * group + h) * HEAD_SIZE : (g * group + h + 1) * HEAD_SIZE].astype(jnp.float32)
            for h in range(group)
        ]
        q = jnp.concatenate(heads, axis=0).astype(jnp.bfloat16)
        qs[g] = q
        key = f_ref[0, :, 2 * g * HEAD_SIZE : (2 * g + 1) * HEAD_SIZE]
        value = f_ref[0, :, (2 * g + 1) * HEAD_SIZE : (2 * g + 2) * HEAD_SIZE]
        s = jnp.where(newer <= token, nt(q, key), MASKED)
        m = jnp.max(s, axis=-1, keepdims=True)
        p = jnp.exp2((s - m) * factor)
        ms[g] = m
        ls[g] = jnp.sum(p, axis=-1, keepdims=True)
        acc[g] = jnp.dot(p.astype(jnp.bfloat16), value, preferred_element_type=jnp.float32)

    def body(at, carry):
        ids = [tab_ref[slot, jnp.minimum(at * PAGE_GROUP + u, maxp - 1)] for u in range(PAGE_GROUP)]
        pos = at * span + lax.broadcasted_iota(jnp.int32, (rows, span), 1)
        valid = pos < length
        def side(g, which):
            first = (2 * g + which) * HEAD_SIZE
            return jnp.concatenate([pages_ref[i, :, first : first + HEAD_SIZE] for i in ids], axis=0)

        def scored(g):
            return jnp.where(valid, nt(qs[g], side(g, 0)), MASKED)

        s = scored(0)
        for g in range(kv_heads):
            following = scored(g + 1) if g + 1 < kv_heads else None
            before = ms[g]
            m = jnp.maximum(before, jnp.max(s, axis=-1, keepdims=True))
            fade = jnp.exp2((before - m) * factor)
            p = jnp.exp2((s - m) * factor)
            ms[g] = m
            ls[g] = ls[g] * fade + jnp.sum(p, axis=-1, keepdims=True)
            acc[g] = acc[g] * fade + jnp.dot(
                p.astype(jnp.bfloat16), side(g, 1), preferred_element_type=jnp.float32
            )
            s = following
        return carry

    lax.fori_loop(0, groups, body, 0)
    for g in range(kv_heads):
        o = acc[g] / ls[g]
        for h in range(group):
            o_ref[0, :, (g * group + h) * HEAD_SIZE : (g * group + h + 1) * HEAD_SIZE] = o[
                h * tokens : (h + 1) * tokens
            ].astype(jnp.bfloat16)


def attend(queries, fresh_kv, pages, lengths, table):
    slots, tokens, width = queries.shape
    kv_heads = fresh_kv.shape[2] // (2 * HEAD_SIZE)
    group = width // (kv_heads * HEAD_SIZE)
    rows = group * tokens
    return pl.pallas_call(
        functools.partial(attend_kernel, kv_heads, group),
        out_shape=jax.ShapeDtypeStruct(queries.shape, jnp.bfloat16),
        grid_spec=pltpu.PrefetchScalarGridSpec(
            num_scalar_prefetch=2,
            grid=(slots,),
            in_specs=[
                pl.BlockSpec((1, tokens, width), lambda s, a, b: (s, 0, 0)),
                pl.BlockSpec((1, tokens, fresh_kv.shape[2]), lambda s, a, b: (s, 0, 0)),
                pl.BlockSpec(pages.shape, lambda s, a, b: (0, 0, 0), pipeline_mode=pl.Buffered(1)),
            ],
            out_specs=pl.BlockSpec((1, tokens, width), lambda s, a, b: (s, 0, 0)),
            scratch_shapes=[
                pltpu.VMEM((kv_heads, rows, HEAD_SIZE), jnp.bfloat16),
                pltpu.VMEM((kv_heads, rows, 1), jnp.float32),
                pltpu.VMEM((kv_heads, rows, 1), jnp.float32),
                pltpu.VMEM((kv_heads, rows, HEAD_SIZE), jnp.float32),
            ],
        ),
        compiler_params=pltpu.CompilerParams(vmem_limit_bytes=40 << 20),
        cost_estimate=pl.CostEstimate(
            flops=4 * rows * kv_heads * pages.shape[0] * pages.shape[1] * HEAD_SIZE,
            transcendentals=rows * kv_heads * pages.shape[0] * pages.shape[1],
            bytes_accessed=pages.size * 2 + queries.size * 4,
        ),
    )(lengths, table, queries, fresh_kv, pages)

MESH = pl.DeviceIdType.MESH
GROUPS = 3
PARTS = 4
PIECES = GROUPS * PARTS
AHEAD = 3
WPARTS = 16
WSENT = (4, 5, 6, 7, 8, 9, 10, 11, 13, 15, 16, 16, 16)
UNITS = 12
LAG = 2
STEP_PAGES = 4
PAGE_COPIES = 4
MOVER_POSITIONS = 512
UNIT_G = (0, 0, 1, 1, 0, 1, 2, 2, 2, 0, 1, 2)
UNIT_F = (0, 0, 0, 0, 1, 1, 0, 0, 1, 1, 1, 1)
UNIT_I = (0, 1, 0, 1, 0, 0, 0, 1, 0, 1, 1, 1)
PASS_FROM, PASS_EVERY = 12, 5


def pick(at, table):
    value = table[0]
    for k in range(1, len(table)):
        if table[k] != table[k - 1]:
            value = jnp.where(at >= k, table[k], value)
    return value


def fused_kernel(
    rank_steps,
    q_any, f_any, pages_any, len_ref, tab_ref, mov_ref, w_ref, o_ref,
    q_ref, f_ref, pages_ref, order_ref, qs, scores, ms, ls, sums, acc, att_ref,
    abuf, wbuf, psend, precv, ploc, csum, obuf,
    in_sem, wl_sem, wz_send, wz_recv, wt_send, wt_recv, a1_send, a2_send, f_send, az_recv, ay_recv,
    x_send, x_recv, o_send0, o_send, o_recv0, o_recv,
):
    me, x = lax.axis_index("req"), lax.axis_index("tp")
    n = 16
    z, y, c = me // 4, (me // 2) % 2, me % 2
    own = z % 2
    oth = 1 - own
    t = z // 2
    inner = jnp.logical_or(z == 1, z == 2)
    outer = jnp.logical_not(inner)
    far = 2 - t
    zp = z + 1 - 2 * own
    keeper = x == t
    mine = 2 * y + own
    kept = jnp.where(keeper, 1 - y, y)
    rows = att_ref.shape[1]
    slots, tokens = q_ref.shape[0], q_ref.shape[1]
    kv_heads, group = qs.shape[0], qs.shape[1] // q_ref.shape[1]
    page = pages_ref.shape[1]
    maxp = tab_ref.shape[1]
    qrows = group * tokens
    factor = HEAD_SIZE ** (-0.5) * LOG2E
    wide = w_ref.shape[0]
    wrows = wide // 2
    cols = att_ref.shape[2] // PARTS

    def at(zz, yy, cc, xx):
        return {"req": zz * 4 + yy * 2 + cc, "tp": xx}

    def remote(src, dst, ss, rs, dev):
        return pltpu.make_async_remote_copy(
            src_ref=src, dst_ref=dst, send_sem=ss, recv_sem=rs, device_id=dev, device_id_type=MESH
        )

    barrier = pltpu.get_barrier_semaphore()
    my_index = me * 2 + x

    def greet(i, carry):
        target = (my_index + i) % (2 * n)
        pl.semaphore_signal(
            barrier, inc=1, device_id={"req": target // 2, "tp": target % 2}, device_id_type=MESH
        )
        return carry

    lax.fori_loop(1, 2 * n, greet, 0)

    def local_w(i):
        return pltpu.make_async_copy(w_ref.at[pl.ds(i * wrows, wrows)], wbuf.at[own, i, c], wl_sem.at[i])

    inputs = [
        pltpu.make_async_copy(q_any, q_ref, in_sem.at[0]),
        pltpu.make_async_copy(f_any, f_ref, in_sem.at[1]),
    ]
    share = pages_any.shape[0] // PAGE_COPIES
    for i in range(PAGE_COPIES):
        part = pl.ds(i * share, share)
        inputs.append(pltpu.make_async_copy(pages_any.at[part], pages_ref.at[part], in_sem.at[2 + i]))
    for copy in inputs:
        copy.start()
    for i in range(2):
        local_w(i).start()

    keys = []
    for slot in range(slots):
        key = len_ref[slot] * slots + slot
        key = jnp.where(mov_ref[0, 1] == slot, -1, key)
        keys.append(jnp.where(mov_ref[0, 0] == slot, -2, key))
    ranks = []
    for slot in range(slots):
        rank = 0
        for i in range(slots):
            if i != slot:
                rank = rank + jnp.where(keys[i] < keys[slot], 1, 0)
        ranks.append(rank)
    for k in range(slots):
        slot_at = 0
        for slot in range(1, slots):
            slot_at = slot_at + jnp.where(ranks[slot] == k, slot, 0)
        order_ref[k] = slot_at
        order_ref[slots + k] = ranks[k]
    pl.semaphore_wait(barrier, 2 * n - 1)

    wpart = wide // WPARTS
    whalf = WPARTS // 2

    def wz(k):
        part = pl.ds(pl.multiple_of(k * wpart, wpart), wpart)
        there = pl.ds(pl.multiple_of(k % whalf * wpart, wpart), wpart)
        return remote(
            w_ref.at[part], wbuf.at[own, k // whalf, c, there], wz_send.at[k], wz_recv.at[k], at(zp, y, c, x)
        )

    def wz_in(k):
        where = wbuf.at[oth, k // whalf, c, pl.ds(pl.multiple_of(k % whalf * wpart, wpart), wpart)]
        return remote(where, where, wz_send.at[k], wz_recv.at[k], at(zp, y, c, x))

    def w_half(i):
        def one(k, carry):
            wz_in(k).wait_recv()
            return carry

        lax.fori_loop(i * whalf, (i + 1) * whalf, one, 0)
        twin(oth, i).start()

    def twin(f, i):
        src = w_ref.at[pl.ds(i * wrows, wrows)] if f is own else wbuf.at[f, i, c]
        return remote(src, wbuf.at[f, i, c], wt_send.at[f, i], wt_recv.at[f, i], at(z, y, 1 - c, x))

    def twin_in(f, i):
        where = wbuf.at[f, i, 1 - c]
        return remote(where, where, wt_send.at[f, i], wt_recv.at[f, i], at(z, y, 1 - c, x))

    token = lax.broadcasted_iota(jnp.int32, (qrows, tokens), 0) % tokens
    newer = lax.broadcasted_iota(jnp.int32, (qrows, tokens), 1)
    span = STEP_PAGES * page

    lanes = (qrows, HEAD_SIZE)

    def fresh_scores(slot, g):
        key = f_ref[slot, :, 2 * g * HEAD_SIZE : (2 * g + 1) * HEAD_SIZE]
        return jnp.where(newer <= token, nt(qs[g], key), MASKED)

    def tiles(a):
        return [a[:, i * HEAD_SIZE : (i + 1) * HEAD_SIZE] for i in range(a.shape[1] // HEAD_SIZE)]

    def attend_start(slot):
        for g in range(kv_heads):
            heads = [
                q_ref[slot, :, (g * group + h) * HEAD_SIZE : (g * group + h + 1) * HEAD_SIZE].astype(jnp.float32)
                for h in range(group)
            ]
            qs[g] = jnp.concatenate(heads, axis=0).astype(jnp.bfloat16)
            ms[g] = jnp.broadcast_to(jnp.max(fresh_scores(slot, g), axis=-1, keepdims=True), lanes)

    def page_side(slot, at_step, g, which):
        first = (2 * g + which) * HEAD_SIZE
        ids = [tab_ref[slot, jnp.minimum(at_step * STEP_PAGES + u, maxp - 1)] for u in range(STEP_PAGES)]
        return jnp.concatenate([pages_ref[i, :, first : first + HEAD_SIZE] for i in ids], axis=0)

    def score_step(slot, at_step):
        pos = at_step * span + lax.broadcasted_iota(jnp.int32, (1, span), 1)
        bias = jnp.where(pos < len_ref[slot], 0.0, MASKED)
        for g in range(kv_heads):
            s = nt(qs[g], page_side(slot, at_step, g, 0)) + bias
            scores[at_step, g] = s
            ms[g] = functools.reduce(jnp.maximum, tiles(s), ms[g])

    def attend_middle(slot, j):
        for g in range(kv_heads):
            m = jnp.max(ms[g], axis=-1, keepdims=True)
            p = jnp.exp2((fresh_scores(slot, g) - m) * factor)
            value = f_ref[slot, :, (2 * g + 1) * HEAD_SIZE : (2 * g + 2) * HEAD_SIZE]
            ms[g] = jnp.broadcast_to(m, lanes)
            ls[j, g] = jnp.sum(p, axis=-1, keepdims=True)
            sums[j, g] = jnp.zeros(lanes, jnp.float32)
            acc[j, g] = jnp.dot(p.astype(jnp.bfloat16), value, preferred_element_type=jnp.float32)

    def value_step(slot, j, at_step):
        for g in range(kv_heads):
            m = ms[g]
            p = [jnp.exp2((a - m) * factor) for a in tiles(scores[at_step, g])]
            sums[j, g] += functools.reduce(jnp.add, p)
            weights = jnp.concatenate(p, axis=1).astype(jnp.bfloat16)
            acc[j, g] += jnp.dot(weights, page_side(slot, at_step, g, 1), preferred_element_type=jnp.float32)

    def finish_group(at_group):
        for g in range(kv_heads):
            o = [acc[j, g] / (ls[j, g] + jnp.sum(sums[j, g], axis=-1, keepdims=True)) for j in range(2)]
            for h in range(group):
                lane = (g * group + h) * HEAD_SIZE
                att_ref[at_group, :, lane : lane + HEAD_SIZE] = jnp.concatenate(
                    [o[j][h * tokens : (h + 1) * tokens] for j in range(2)], axis=0
                ).astype(jnp.bfloat16)

        @pl.when(outer)
        def _():
            abuf[at_group, mine] = att_ref[at_group]

    def rows_of(p):
        return att_ref.at[p // PARTS, :, pl.ds(pl.multiple_of((p % PARTS) * cols, cols), cols)]

    def place(p, s):
        return abuf.at[p // PARTS, s, :, pl.ds(pl.multiple_of((p % PARTS) * cols, cols), cols)]

    def a1_outer(p):
        return remote(rows_of(p), place(p, mine), a1_send.at[p], ay_recv.at[p, own], at(z, 1 - y, c, x))

    def a1_inner(p):
        return remote(rows_of(p), place(p, mine), a1_send.at[p], az_recv.at[p, own], at(zp, y, c, x))

    def a2(p):
        return remote(rows_of(p), place(p, mine), a2_send.at[p], az_recv.at[p, own], at(far, y, c, x))

    def z_in(p, q):
        where = place(p, 2 * y + q)
        return remote(where, where, a1_send.at[p], az_recv.at[p, q], at(zp, y, c, x))

    def forward(p, q):
        where = place(p, 2 * y + q)
        return remote(where, where, f_send.at[p, q], ay_recv.at[p, q], at(z, 1 - y, c, x))

    def y_in(p, q):
        where = place(p, 2 * (1 - y) + q)
        return remote(where, where, f_send.at[p, q], ay_recv.at[p, q], at(z, 1 - y, c, x))

    def send_rows(p):
        a2(p).start()

        @pl.when(inner)
        def _():
            a1_inner(p).start()

        @pl.when(outer)
        def _():
            a1_outer(p).start()

    def rows_left(p):
        a2(p).wait_send()
        a1_inner(p).wait_send()

    def pass_on(p):
        z_in(p, oth).wait_recv()
        forward(p, oth).start()

        @pl.when(inner)
        def _():
            z_in(p, own).wait_recv()
            forward(p, own).start()

        @pl.when(p < PIECES - AHEAD)
        def _():
            rows_left(p)
            send_rows(p + AHEAD)

        def one(k, carry):
            wz(k).start()
            return carry

        lax.fori_loop(pick(p, WSENT), pick(p, WSENT[1:]), one, 0)

    def forwarded(g):
        def one(h, carry):
            for q in range(2):
                y_in(g * PARTS + h, q).wait_recv()
            return carry

        lax.fori_loop(0, PARTS, one, 0)

    def unit(u):
        f = pick(u, UNIT_F)
        return pick(u, UNIT_G), jnp.where(f == 0, own, oth), pick(u, UNIT_I)

    def x_copy(g, f, i):
        return remote(
            psend.at[g, f, i], precv.at[g, f, i], x_send.at[g, f, i], x_recv.at[g, f, i], at(z, y, c, 1 - x)
        )

    def compute(u):
        g, f, i = unit(u)
        a = abuf[g].reshape(4 * rows, abuf.shape[3])
        part = nt(a, wbuf[f, i].reshape(2 * wrows, wbuf.shape[4]))

        low, high = part[: 2 * rows], part[2 * rows :]
        first = kept == 0
        ploc[g, f, i] = jnp.where(first, low, high)
        psend[g, f, i] = jnp.where(first, high, low).astype(jnp.bfloat16)
        x_copy(g, f, i).start()

    def out0(j, q, f, i):
        r = (2 * own + q) * 4 + kept * 2 + c
        dest = (r + n + 1 - 2 * j) % n
        return remote(
            csum.at[q, f, i, j], obuf.at[y, f, i, j], o_send0.at[j, q, f, i], o_recv0.at[j, y, f, i],
            {"req": dest, "tp": t},
        )

    def out(g, q, f, i):
        pair = pl.ds(2 * g, 2)
        return remote(
            csum.at[q, f, i, pair], obuf.at[y, f, i, pair], o_send.at[g - 1, q, f, i],
            o_recv.at[g - 1, y, f, i], at(2 * own + q, kept, c, t),
        )

    half = rows // 2

    def reduce(u):
        g, f, i = unit(u)
        x_copy(g, f, i).wait_recv()
        for q in range(2):
            total = ploc[g, f, i, q * rows : (q + 1) * rows] + precv[g, f, i, q * rows : (q + 1) * rows].astype(
                jnp.float32
            )
            for j in range(2):
                csum[q, f, i, 2 * g + j] = total[j * half : (j + 1) * half].astype(jnp.bfloat16)

        @pl.when(g == 0)
        def _():
            for q in range(2):
                for j in range(2):
                    out0(j, q, f, i).start()

        @pl.when(g > 0)
        def _():
            for q in range(2):
                out(g, q, f, i).start()

    for k in range(WSENT[0]):
        wz(k).start()
    for copy in inputs:
        copy.wait()

    ranks_at, starts, ends, tops = [], [], [], []
    for k, steps in enumerate(rank_steps):
        starts += [len(ranks_at)] * 2 * steps
        tops += [steps] * 2 * steps
        ranks_at += [k] * 2 * steps
        ends.append(len(ranks_at) - 1)

    def pass_loop(p, carry):
        pass_on(p)
        return carry

    passed = [0]
    for tick in range(len(ranks_at)):
        ready = PARTS * sum(tick >= e for e in ends[1::2])
        due = max(0, (tick - PASS_FROM) // PASS_EVERY + 1)
        passed.append(max(passed[-1], min(due, ready - AHEAD, PIECES - 2)))

    def attend_loop(tick, carry):
        k = pick(tick, ranks_at)
        top = pick(tick, tops)
        in_rank = tick - pick(tick, starts)
        slot = order_ref[k]
        j = k % 2

        @pl.when(in_rank == 0)
        def _():
            attend_start(slot)

        @pl.when(in_rank < top)
        def _():
            score_step(slot, in_rank)

        @pl.when(in_rank == top)
        def _():
            attend_middle(slot, j)

        @pl.when(in_rank >= top)
        def _():
            value_step(slot, j, in_rank - top)

        @pl.when(functools.reduce(jnp.logical_or, [tick == e for e in ends[1::2]]))
        def _():
            finish_group(k // 2)

        @pl.when(tick == ends[1])
        def _():
            for p in range(AHEAD):
                send_rows(p)
            for i in range(2):
                local_w(i).wait()
                twin(own, i).start()

        lax.fori_loop(pick(tick, passed), pick(tick, passed[1:]), pass_loop, 0)
        return carry

    lax.fori_loop(0, len(ranks_at), attend_loop, 0)

    def step(u, carry):
        @pl.when(u == 0)
        def _():
            for i in range(2):
                twin_in(own, i).wait_recv()
            lax.fori_loop(passed[-1], max(passed[-1], PARTS), pass_loop, 0)
            forwarded(0)

        @pl.when(u == 2)
        def _():
            lax.fori_loop(max(passed[-1], PARTS), PIECES - 2, pass_loop, 0)
            forwarded(1)

        @pl.when(u == 4)
        def _():
            w_half(0)
            twin_in(oth, 0).wait_recv()

        @pl.when(u == 6)
        def _():
            lax.fori_loop(PIECES - 2, PIECES, pass_loop, 0)
            forwarded(2)

        @pl.when(u == 9)
        def _():
            w_half(1)
            twin_in(oth, 1).wait_recv()

        compute(u)

        @pl.when(u >= LAG)
        def _():
            reduce(u - LAG)

        return carry

    lax.fori_loop(0, UNITS, step, 0)
    for u in range(UNITS - LAG, UNITS):
        reduce(u)

    def weights_left(k, carry):
        wz(k).wait_send()
        return carry

    lax.fori_loop(0, WPARTS, weights_left, 0)
    for i in range(2):
        twin(own, i).wait_send()
        twin(oth, i).wait_send()

    def passed(p, carry):
        @pl.when(p >= PIECES - AHEAD)
        def _():
            rows_left(p)

        forward(p, oth).wait_send()

        @pl.when(inner)
        def _():
            forward(p, own).wait_send()

        return carry

    lax.fori_loop(0, PIECES, passed, 0)

    def sent(u, carry):
        g, f, i = unit(u)

        x_copy(g, f, i).wait_send()

        @pl.when(g == 0)
        def _():
            for q in range(2):
                for j in range(2):
                    out0(j, q, f, i).wait_send()

        @pl.when(g > 0)
        def _():
            for q in range(2):
                out(g, q, f, i).wait_send()

        return carry

    lax.fori_loop(0, UNITS, sent, 0)

    def columns(f, yy, i, cc):
        first = f * 4 * wide + yy * 2 * wide + cc * wide + i * wrows
        return slice(first, first + wrows)

    for f in range(2):
        for i in range(2):
            for yy in range(2):
                for j in range(2):
                    remote(
                        csum.at[0, 0, 0, 0], obuf.at[yy, f, i, j], o_send0.at[0, 0, 0, 0],
                        o_recv0.at[j, yy, f, i], at(z, y, 1 - c, x),
                    ).wait_recv()
                for g in range(1, GROUPS):
                    remote(
                        csum.at[0, 0, 0, pl.ds(0, 2)], obuf.at[yy, f, i, pl.ds(2 * g, 2)], o_send.at[0, 0, 0, 0],
                        o_recv.at[g - 1, yy, f, i], at(z, y, 1 - c, x),
                    ).wait_recv()

    for slot in range(slots):
        rank = order_ref[slots + slot]
        for f in range(2):
            for i in range(2):
                for yy in range(2):
                    for cc in range(2):
                        o_ref[slot, :, columns(f, yy, i, cc)] = obuf[
                            yy, f, i, rank, :, cc * wrows : (cc + 1) * wrows
                        ]


def fused(queries, fresh_kv, pages, lengths, table, movers, w_out):
    slots, tokens, width = queries.shape
    wide = w_out.shape[0]
    kv_heads = fresh_kv.shape[2] // (2 * HEAD_SIZE)
    qrows = width // (kv_heads * HEAD_SIZE) * tokens
    rows = slots * tokens // GROUPS
    pool, page, maxp = pages.shape[0], pages.shape[1], table.shape[1]
    most = [-(-MOVER_POSITIONS // page)] * 2
    for i in range(slots - 2):
        most.append(min(maxp, (pool - 2 - i) // (slots - 2 - i)))
    rank_steps = tuple(-(-m // STEP_PAGES) for m in most)
    dma = pltpu.SemaphoreType.DMA
    smem, hbm = pl.BlockSpec(memory_space=pltpu.SMEM), pl.BlockSpec(memory_space=pl.ANY)
    b, f32 = jnp.bfloat16, jnp.float32
    done = pl.pallas_call(
        functools.partial(fused_kernel, rank_steps),
        out_shape=jax.ShapeDtypeStruct((slots, tokens, 8 * wide), b),
        in_specs=[hbm, hbm, hbm, smem, smem, smem, hbm],
        out_specs=pl.BlockSpec(memory_space=pltpu.VMEM),
        scratch_shapes=[
            pltpu.VMEM(queries.shape, b),
            pltpu.VMEM(fresh_kv.shape, b),
            pltpu.VMEM(pages.shape, b),
            pltpu.SMEM((2 * slots,), jnp.int32),
            pltpu.VMEM((kv_heads, qrows, HEAD_SIZE), b),
            pltpu.VMEM((max(rank_steps), kv_heads, qrows, STEP_PAGES * page), f32),
            pltpu.VMEM((kv_heads, qrows, HEAD_SIZE), f32),
            pltpu.VMEM((2, kv_heads, qrows, 1), f32),
            pltpu.VMEM((2, kv_heads, qrows, HEAD_SIZE), f32),
            pltpu.VMEM((2, kv_heads, qrows, HEAD_SIZE), f32),
            pltpu.VMEM((GROUPS, rows, width), b),
            pltpu.VMEM((GROUPS, 4, rows, width), b),
            pltpu.VMEM((2, 2, 2, wide // 2, width), b),
            pltpu.VMEM((GROUPS, 2, 2, 2 * rows, wide), b),
            pltpu.VMEM((GROUPS, 2, 2, 2 * rows, wide), b),
            pltpu.VMEM((GROUPS, 2, 2, 2 * rows, wide), f32),
            pltpu.VMEM((2, 2, 2, slots, tokens, wide), b),
            pltpu.VMEM((2, 2, 2, slots, tokens, wide), b),
            dma((2 + PAGE_COPIES,)), dma((2,)), dma((WPARTS,)), dma((WPARTS,)), dma((2, 2)), dma((2, 2)),
            dma((PIECES,)), dma((PIECES,)), dma((PIECES, 2)), dma((PIECES, 2)), dma((PIECES, 2)),
            dma((GROUPS, 2, 2)), dma((GROUPS, 2, 2)),
            dma((2, 2, 2, 2)), dma((GROUPS - 1, 2, 2, 2)), dma((2, 2, 2, 2)), dma((GROUPS - 1, 2, 2, 2)),
        ],
        compiler_params=pltpu.CompilerParams(
            collective_id=0, has_side_effects=True, vmem_limit_bytes=60 << 20
        ),
    )(queries, fresh_kv, pages, lengths, table, movers, w_out)
    return done.reshape(slots * tokens, 8 * wide)


def per_device(queries, fresh_kv, key_value_pages, cache_lengths, page_table, movers, w_out):
    slots, tokens, width = queries.shape
    to_next = movers[0, 0]
    to_prev = movers[0, 1]
    if lax.axis_size("tp") == 2 and lax.axis_size("req") == 16 and slots == 2 * GROUPS and key_value_pages.shape[0] % PAGE_COPIES == 0:
        return fused(queries, fresh_kv, key_value_pages, cache_lengths, page_table, movers, w_out)
    attended = attend(queries, fresh_kv, key_value_pages, cache_lengths, page_table)
    from_left = passed_along(attended[to_next], "req", 1)
    from_right = passed_along(attended[to_prev], "req", -1)
    slot_ids = jnp.arange(slots, dtype=jnp.int32)[:, None, None]
    placed = jnp.where(
        slot_ids == to_next, from_left[None], jnp.where(slot_ids == to_prev, from_right[None], attended)
    )
    flat = placed.reshape(slots * tokens, width)
    partial_sum = lax.dot_general(
        flat,
        lax.all_gather(w_out, "req", axis=0, tiled=True),
        (((1,), (1,)), ((), ())),
        preferred_element_type=jnp.float32,
    )
    return lax.psum_scatter(partial_sum, "tp", scatter_dimension=1, tiled=True).astype(jnp.bfloat16)


def solution(mesh):
    return jax.shard_map(
        per_device,
        mesh=mesh,
        in_specs=(
            P("req", None, "tp"),
            P("req", None, "tp"),
            P("req", None, "tp"),
            P("req"),
            P("req", None),
            P("req", None),
            P("req", "tp"),
        ),
        out_specs=P("req", "tp"),
        check_vma=False,
    )
```

```python
import functools

import jax
import jax.numpy as jnp
from jax import lax
from jax.experimental import pallas as pl
from jax.experimental.pallas import tpu as pltpu
from jax.sharding import PartitionSpec as P

HEAD_SIZE = 128
PAGE_GROUP = 8
LOG2E = 1.4426950408889634
MASKED = -1e30


def passed_along(block, axis, distance):
    devices = range(lax.axis_size(axis))
    route = [((i - distance) % len(devices), i) for i in devices]
    return lax.ppermute(block, axis, route)


def nt(a, b):
    return lax.dot_general(a, b, (((1,), (1,)), ((), ())), preferred_element_type=jnp.float32)


def attend_kernel(kv_heads, group, len_ref, tab_ref, q_ref, f_ref, pages_ref, o_ref, qs, ms, ls, acc):
    slot = pl.program_id(0)
    tokens = q_ref.shape[1]
    page = pages_ref.shape[1]
    rows = group * tokens
    maxp = tab_ref.shape[1]
    length = len_ref[slot]
    factor = HEAD_SIZE ** (-0.5) * LOG2E
    span = PAGE_GROUP * page
    groups = (length + span - 1) // span
    token = lax.broadcasted_iota(jnp.int32, (rows, tokens), 0) % tokens
    newer = lax.broadcasted_iota(jnp.int32, (rows, tokens), 1)
    for g in range(kv_heads):
        heads = [
            q_ref[0, :, (g * group + h) * HEAD_SIZE : (g * group + h + 1) * HEAD_SIZE].astype(jnp.float32)
            for h in range(group)
        ]
        q = jnp.concatenate(heads, axis=0).astype(jnp.bfloat16)
        qs[g] = q
        key = f_ref[0, :, 2 * g * HEAD_SIZE : (2 * g + 1) * HEAD_SIZE]
        value = f_ref[0, :, (2 * g + 1) * HEAD_SIZE : (2 * g + 2) * HEAD_SIZE]
        s = jnp.where(newer <= token, nt(q, key), MASKED)
        m = jnp.max(s, axis=-1, keepdims=True)
        p = jnp.exp2((s - m) * factor)
        ms[g] = m
        ls[g] = jnp.sum(p, axis=-1, keepdims=True)
        acc[g] = jnp.dot(p.astype(jnp.bfloat16), value, preferred_element_type=jnp.float32)

    def body(at, carry):
        ids = [tab_ref[slot, jnp.minimum(at * PAGE_GROUP + u, maxp - 1)] for u in range(PAGE_GROUP)]
        pos = at * span + lax.broadcasted_iota(jnp.int32, (rows, span), 1)
        valid = pos < length
        def side(g, which):
            first = (2 * g + which) * HEAD_SIZE
            return jnp.concatenate([pages_ref[i, :, first : first + HEAD_SIZE] for i in ids], axis=0)

        def scored(g):
            return jnp.where(valid, nt(qs[g], side(g, 0)), MASKED)

        s = scored(0)
        for g in range(kv_heads):
            following = scored(g + 1) if g + 1 < kv_heads else None
            before = ms[g]
            m = jnp.maximum(before, jnp.max(s, axis=-1, keepdims=True))
            fade = jnp.exp2((before - m) * factor)
            p = jnp.exp2((s - m) * factor)
            ms[g] = m
            ls[g] = ls[g] * fade + jnp.sum(p, axis=-1, keepdims=True)
            acc[g] = acc[g] * fade + jnp.dot(
                p.astype(jnp.bfloat16), side(g, 1), preferred_element_type=jnp.float32
            )
            s = following
        return carry

    lax.fori_loop(0, groups, body, 0)
    for g in range(kv_heads):
        o = acc[g] / ls[g]
        for h in range(group):
            o_ref[0, :, (g * group + h) * HEAD_SIZE : (g * group + h + 1) * HEAD_SIZE] = o[
                h * tokens : (h + 1) * tokens
            ].astype(jnp.bfloat16)


def attend(queries, fresh_kv, pages, lengths, table):
    slots, tokens, width = queries.shape
    kv_heads = fresh_kv.shape[2] // (2 * HEAD_SIZE)
    group = width // (kv_heads * HEAD_SIZE)
    rows = group * tokens
    return pl.pallas_call(
        functools.partial(attend_kernel, kv_heads, group),
        out_shape=jax.ShapeDtypeStruct(queries.shape, jnp.bfloat16),
        grid_spec=pltpu.PrefetchScalarGridSpec(
            num_scalar_prefetch=2,
            grid=(slots,),
            in_specs=[
                pl.BlockSpec((1, tokens, width), lambda s, a, b: (s, 0, 0)),
                pl.BlockSpec((1, tokens, fresh_kv.shape[2]), lambda s, a, b: (s, 0, 0)),
                pl.BlockSpec(pages.shape, lambda s, a, b: (0, 0, 0), pipeline_mode=pl.Buffered(1)),
            ],
            out_specs=pl.BlockSpec((1, tokens, width), lambda s, a, b: (s, 0, 0)),
            scratch_shapes=[
                pltpu.VMEM((kv_heads, rows, HEAD_SIZE), jnp.bfloat16),
                pltpu.VMEM((kv_heads, rows, 1), jnp.float32),
                pltpu.VMEM((kv_heads, rows, 1), jnp.float32),
                pltpu.VMEM((kv_heads, rows, HEAD_SIZE), jnp.float32),
            ],
        ),
        compiler_params=pltpu.CompilerParams(vmem_limit_bytes=40 << 20),
        cost_estimate=pl.CostEstimate(
            flops=4 * rows * kv_heads * pages.shape[0] * pages.shape[1] * HEAD_SIZE,
            transcendentals=rows * kv_heads * pages.shape[0] * pages.shape[1],
            bytes_accessed=pages.size * 2 + queries.size * 4,
        ),
    )(lengths, table, queries, fresh_kv, pages)

MESH = pl.DeviceIdType.MESH
GROUPS = 3
PARTS = 4
PIECES = GROUPS * PARTS
AHEAD = 3
WPARTS = 16
WSENT = (4, 5, 6, 7, 8, 9, 10, 11, 13, 15, 16, 16, 16)
UNITS = 12
LAG = 3
STEP_PAGES = 4
PAGE_COPIES = 4
MOVER_POSITIONS = 512
UNIT_G = (0, 0, 1, 1, 0, 1, 2, 2, 2, 0, 1, 2)
UNIT_F = (0, 0, 0, 0, 1, 1, 0, 0, 1, 1, 1, 1)
UNIT_I = (0, 1, 0, 1, 0, 0, 0, 1, 0, 1, 1, 1)
PASS_FROM, PASS_EVERY = 12, 5


def pick(at, table):
    value = table[0]
    for k in range(1, len(table)):
        if table[k] != table[k - 1]:
            value = jnp.where(at >= k, table[k], value)
    return value


def fused_kernel(
    rank_steps,
    q_any, f_any, pages_any, len_ref, tab_ref, mov_ref, w_ref, o_ref,
    q_ref, f_ref, pages_ref, order_ref, qs, scores, ms, ls, sums, acc, att_ref,
    abuf, wbuf, psend, precv, ploc, csum, obuf,
    in_sem, wl_sem, wz_send, wz_recv, wt_send, wt_recv, a1_send, a2_send, f_send, az_recv, ay_recv,
    x_send, x_recv, o_send0, o_send, o_recv0, o_recv,
):
    me, x = lax.axis_index("req"), lax.axis_index("tp")
    n = 16
    z, y, c = me // 4, (me // 2) % 2, me % 2
    own = z % 2
    oth = 1 - own
    t = z // 2
    inner = jnp.logical_or(z == 1, z == 2)
    outer = jnp.logical_not(inner)
    far = 2 - t
    zp = z + 1 - 2 * own
    keeper = x == t
    mine = 2 * y + own
    kept = jnp.where(keeper, 1 - y, y)
    rows = att_ref.shape[1]
    slots, tokens = q_ref.shape[0], q_ref.shape[1]
    kv_heads, group = qs.shape[0], qs.shape[1] // q_ref.shape[1]
    page = pages_ref.shape[1]
    maxp = tab_ref.shape[1]
    qrows = group * tokens
    factor = HEAD_SIZE ** (-0.5) * LOG2E
    wide = w_ref.shape[0]
    wrows = wide // 2
    cols = att_ref.shape[2] // PARTS

    def at(zz, yy, cc, xx):
        return {"req": zz * 4 + yy * 2 + cc, "tp": xx}

    def remote(src, dst, ss, rs, dev):
        return pltpu.make_async_remote_copy(
            src_ref=src, dst_ref=dst, send_sem=ss, recv_sem=rs, device_id=dev, device_id_type=MESH
        )

    barrier = pltpu.get_barrier_semaphore()
    my_index = me * 2 + x

    def greet(i, carry):
        target = (my_index + i) % (2 * n)
        pl.semaphore_signal(
            barrier, inc=1, device_id={"req": target // 2, "tp": target % 2}, device_id_type=MESH
        )
        return carry

    lax.fori_loop(1, 2 * n, greet, 0)

    def local_w(i):
        return pltpu.make_async_copy(w_ref.at[pl.ds(i * wrows, wrows)], wbuf.at[own, i, c], wl_sem.at[i])

    inputs = [
        pltpu.make_async_copy(q_any, q_ref, in_sem.at[0]),
        pltpu.make_async_copy(f_any, f_ref, in_sem.at[1]),
    ]
    share = pages_any.shape[0] // PAGE_COPIES
    for i in range(PAGE_COPIES):
        part = pl.ds(i * share, share)
        inputs.append(pltpu.make_async_copy(pages_any.at[part], pages_ref.at[part], in_sem.at[2 + i]))
    for copy in inputs:
        copy.start()
    for i in range(2):
        local_w(i).start()

    keys = []
    for slot in range(slots):
        key = len_ref[slot] * slots + slot
        key = jnp.where(mov_ref[0, 1] == slot, -1, key)
        keys.append(jnp.where(mov_ref[0, 0] == slot, -2, key))
    ranks = []
    for slot in range(slots):
        rank = 0
        for i in range(slots):
            if i != slot:
                rank = rank + jnp.where(keys[i] < keys[slot], 1, 0)
        ranks.append(rank)
    for k in range(slots):
        slot_at = 0
        for slot in range(1, slots):
            slot_at = slot_at + jnp.where(ranks[slot] == k, slot, 0)
        order_ref[k] = slot_at
        order_ref[slots + k] = ranks[k]
    pl.semaphore_wait(barrier, 2 * n - 1)

    wpart = wide // WPARTS
    whalf = WPARTS // 2

    def wz(k):
        part = pl.ds(pl.multiple_of(k * wpart, wpart), wpart)
        there = pl.ds(pl.multiple_of(k % whalf * wpart, wpart), wpart)
        return remote(
            w_ref.at[part], wbuf.at[own, k // whalf, c, there], wz_send.at[k], wz_recv.at[k], at(zp, y, c, x)
        )

    def wz_in(k):
        where = wbuf.at[oth, k // whalf, c, pl.ds(pl.multiple_of(k % whalf * wpart, wpart), wpart)]
        return remote(where, where, wz_send.at[k], wz_recv.at[k], at(zp, y, c, x))

    def w_half(i):
        def one(k, carry):
            wz_in(k).wait_recv()
            return carry

        lax.fori_loop(i * whalf, (i + 1) * whalf, one, 0)
        twin(oth, i).start()

    def twin(f, i):
        src = w_ref.at[pl.ds(i * wrows, wrows)] if f is own else wbuf.at[f, i, c]
        return remote(src, wbuf.at[f, i, c], wt_send.at[f, i], wt_recv.at[f, i], at(z, y, 1 - c, x))

    def twin_in(f, i):
        where = wbuf.at[f, i, 1 - c]
        return remote(where, where, wt_send.at[f, i], wt_recv.at[f, i], at(z, y, 1 - c, x))

    token = lax.broadcasted_iota(jnp.int32, (qrows, tokens), 0) % tokens
    newer = lax.broadcasted_iota(jnp.int32, (qrows, tokens), 1)
    span = STEP_PAGES * page

    lanes = (qrows, HEAD_SIZE)

    def fresh_scores(slot, g):
        key = f_ref[slot, :, 2 * g * HEAD_SIZE : (2 * g + 1) * HEAD_SIZE]
        return jnp.where(newer <= token, nt(qs[g], key), MASKED)

    def tiles(a):
        return [a[:, i * HEAD_SIZE : (i + 1) * HEAD_SIZE] for i in range(a.shape[1] // HEAD_SIZE)]

    def attend_start(slot):
        for g in range(kv_heads):
            heads = [
                q_ref[slot, :, (g * group + h) * HEAD_SIZE : (g * group + h + 1) * HEAD_SIZE].astype(jnp.float32)
                for h in range(group)
            ]
            qs[g] = jnp.concatenate(heads, axis=0).astype(jnp.bfloat16)
            ms[g] = jnp.broadcast_to(jnp.max(fresh_scores(slot, g), axis=-1, keepdims=True), lanes)

    def page_side(slot, at_step, g, which):
        first = (2 * g + which) * HEAD_SIZE
        ids = [tab_ref[slot, jnp.minimum(at_step * STEP_PAGES + u, maxp - 1)] for u in range(STEP_PAGES)]
        return jnp.concatenate([pages_ref[i, :, first : first + HEAD_SIZE] for i in ids], axis=0)

    def score_step(slot, at_step):
        pos = at_step * span + lax.broadcasted_iota(jnp.int32, (1, span), 1)
        bias = jnp.where(pos < len_ref[slot], 0.0, MASKED)
        for g in range(kv_heads):
            s = nt(qs[g], page_side(slot, at_step, g, 0)) + bias
            scores[at_step, g] = s
            ms[g] = functools.reduce(jnp.maximum, tiles(s), ms[g])

    def attend_middle(slot, j):
        for g in range(kv_heads):
            m = jnp.max(ms[g], axis=-1, keepdims=True)
            p = jnp.exp2((fresh_scores(slot, g) - m) * factor)
            value = f_ref[slot, :, (2 * g + 1) * HEAD_SIZE : (2 * g + 2) * HEAD_SIZE]
            ms[g] = jnp.broadcast_to(m, lanes)
            ls[j, g] = jnp.sum(p, axis=-1, keepdims=True)
            sums[j, g] = jnp.zeros(lanes, jnp.float32)
            acc[j, g] = jnp.dot(p.astype(jnp.bfloat16), value, preferred_element_type=jnp.float32)

    def value_step(slot, j, at_step):
        for g in range(kv_heads):
            m = ms[g]
            p = [jnp.exp2((a - m) * factor) for a in tiles(scores[at_step, g])]
            sums[j, g] += functools.reduce(jnp.add, p)
            weights = jnp.concatenate(p, axis=1).astype(jnp.bfloat16)
            acc[j, g] += jnp.dot(weights, page_side(slot, at_step, g, 1), preferred_element_type=jnp.float32)

    def finish_group(at_group):
        for g in range(kv_heads):
            o = [acc[j, g] / (ls[j, g] + jnp.sum(sums[j, g], axis=-1, keepdims=True)) for j in range(2)]
            for h in range(group):
                lane = (g * group + h) * HEAD_SIZE
                att_ref[at_group, :, lane : lane + HEAD_SIZE] = jnp.concatenate(
                    [o[j][h * tokens : (h + 1) * tokens] for j in range(2)], axis=0
                ).astype(jnp.bfloat16)

        @pl.when(outer)
        def _():
            abuf[at_group, mine] = att_ref[at_group]

    def rows_of(p):
        return att_ref.at[p // PARTS, :, pl.ds(pl.multiple_of((p % PARTS) * cols, cols), cols)]

    def place(p, s):
        return abuf.at[p // PARTS, s, :, pl.ds(pl.multiple_of((p % PARTS) * cols, cols), cols)]

    def a1_outer(p):
        return remote(rows_of(p), place(p, mine), a1_send.at[p], ay_recv.at[p, own], at(z, 1 - y, c, x))

    def a1_inner(p):
        return remote(rows_of(p), place(p, mine), a1_send.at[p], az_recv.at[p, own], at(zp, y, c, x))

    def a2(p):
        return remote(rows_of(p), place(p, mine), a2_send.at[p], az_recv.at[p, own], at(far, y, c, x))

    def z_in(p, q):
        where = place(p, 2 * y + q)
        return remote(where, where, a1_send.at[p], az_recv.at[p, q], at(zp, y, c, x))

    def forward(p, q):
        where = place(p, 2 * y + q)
        return remote(where, where, f_send.at[p, q], ay_recv.at[p, q], at(z, 1 - y, c, x))

    def y_in(p, q):
        where = place(p, 2 * (1 - y) + q)
        return remote(where, where, f_send.at[p, q], ay_recv.at[p, q], at(z, 1 - y, c, x))

    def send_rows(p):
        a2(p).start()

        @pl.when(inner)
        def _():
            a1_inner(p).start()

        @pl.when(outer)
        def _():
            a1_outer(p).start()

    def rows_left(p):
        a2(p).wait_send()
        a1_inner(p).wait_send()

    def pass_on(p):
        z_in(p, oth).wait_recv()
        forward(p, oth).start()

        @pl.when(inner)
        def _():
            z_in(p, own).wait_recv()
            forward(p, own).start()

        @pl.when(p < PIECES - AHEAD)
        def _():
            rows_left(p)
            send_rows(p + AHEAD)

        def one(k, carry):
            wz(k).start()
            return carry

        lax.fori_loop(pick(p, WSENT), pick(p, WSENT[1:]), one, 0)

    def forwarded(g):
        def one(h, carry):
            for q in range(2):
                y_in(g * PARTS + h, q).wait_recv()
            return carry

        lax.fori_loop(0, PARTS, one, 0)

    def unit(u):
        f = pick(u, UNIT_F)
        return pick(u, UNIT_G), jnp.where(f == 0, own, oth), pick(u, UNIT_I)

    def x_copy(g, f, i):
        return remote(
            psend.at[g, f, i], precv.at[g, f, i], x_send.at[g, f, i], x_recv.at[g, f, i], at(z, y, c, 1 - x)
        )

    def compute(u):
        g, f, i = unit(u)
        a = abuf[g].reshape(4 * rows, abuf.shape[3])
        part = nt(a, wbuf[f, i].reshape(2 * wrows, wbuf.shape[4]))

        low, high = part[: 2 * rows], part[2 * rows :]
        first = kept == 0
        ploc[g, f, i] = jnp.where(first, low, high)
        psend[g, f, i] = jnp.where(first, high, low).astype(jnp.bfloat16)
        x_copy(g, f, i).start()

    def out0(j, q, f, i):
        r = (2 * own + q) * 4 + kept * 2 + c
        dest = (r + n + 1 - 2 * j) % n
        return remote(
            csum.at[q, f, i, j], obuf.at[y, f, i, j], o_send0.at[j, q, f, i], o_recv0.at[j, y, f, i],
            {"req": dest, "tp": t},
        )

    def out(g, q, f, i):
        pair = pl.ds(2 * g, 2)
        return remote(
            csum.at[q, f, i, pair], obuf.at[y, f, i, pair], o_send.at[g - 1, q, f, i],
            o_recv.at[g - 1, y, f, i], at(2 * own + q, kept, c, t),
        )

    half = rows // 2

    def reduce(u):
        g, f, i = unit(u)
        x_copy(g, f, i).wait_recv()
        for q in range(2):
            total = ploc[g, f, i, q * rows : (q + 1) * rows] + precv[g, f, i, q * rows : (q + 1) * rows].astype(
                jnp.float32
            )
            for j in range(2):
                csum[q, f, i, 2 * g + j] = total[j * half : (j + 1) * half].astype(jnp.bfloat16)

        @pl.when(g == 0)
        def _():
            for q in range(2):
                for j in range(2):
                    out0(j, q, f, i).start()

        @pl.when(g > 0)
        def _():
            for q in range(2):
                out(g, q, f, i).start()

    for k in range(WSENT[0]):
        wz(k).start()
    for copy in inputs:
        copy.wait()

    ranks_at, starts, ends, tops = [], [], [], []
    for k, steps in enumerate(rank_steps):
        starts += [len(ranks_at)] * 2 * steps
        tops += [steps] * 2 * steps
        ranks_at += [k] * 2 * steps
        ends.append(len(ranks_at) - 1)

    def pass_loop(p, carry):
        pass_on(p)
        return carry

    passed = [0]
    for tick in range(len(ranks_at)):
        ready = PARTS * sum(tick >= e for e in ends[1::2])
        due = max(0, (tick - PASS_FROM) // PASS_EVERY + 1)
        passed.append(max(passed[-1], min(due, ready - AHEAD, PIECES - 2)))

    def attend_loop(tick, carry):
        k = pick(tick, ranks_at)
        top = pick(tick, tops)
        in_rank = tick - pick(tick, starts)
        slot = order_ref[k]
        j = k % 2

        @pl.when(in_rank == 0)
        def _():
            attend_start(slot)

        @pl.when(in_rank < top)
        def _():
            score_step(slot, in_rank)

        @pl.when(in_rank == top)
        def _():
            attend_middle(slot, j)

        @pl.when(in_rank >= top)
        def _():
            value_step(slot, j, in_rank - top)

        @pl.when(functools.reduce(jnp.logical_or, [tick == e for e in ends[1::2]]))
        def _():
            finish_group(k // 2)

        @pl.when(tick == ends[1])
        def _():
            for p in range(AHEAD):
                send_rows(p)
            for i in range(2):
                local_w(i).wait()
                twin(own, i).start()

        lax.fori_loop(pick(tick, passed), pick(tick, passed[1:]), pass_loop, 0)
        return carry

    lax.fori_loop(0, len(ranks_at), attend_loop, 0)

    def step(u, carry):
        @pl.when(u == 0)
        def _():
            for i in range(2):
                twin_in(own, i).wait_recv()
            lax.fori_loop(passed[-1], max(passed[-1], PARTS), pass_loop, 0)
            forwarded(0)

        @pl.when(u == 2)
        def _():
            lax.fori_loop(max(passed[-1], PARTS), PIECES - 2, pass_loop, 0)
            forwarded(1)

        @pl.when(u == 4)
        def _():
            w_half(0)
            twin_in(oth, 0).wait_recv()

        @pl.when(u == 6)
        def _():
            lax.fori_loop(PIECES - 2, PIECES, pass_loop, 0)
            forwarded(2)

        @pl.when(u == 9)
        def _():
            w_half(1)
            twin_in(oth, 1).wait_recv()

        compute(u)

        @pl.when(u >= LAG)
        def _():
            reduce(u - LAG)

        return carry

    lax.fori_loop(0, UNITS, step, 0)
    for u in range(UNITS - LAG, UNITS):
        reduce(u)

    def weights_left(k, carry):
        wz(k).wait_send()
        return carry

    lax.fori_loop(0, WPARTS, weights_left, 0)
    for i in range(2):
        twin(own, i).wait_send()
        twin(oth, i).wait_send()

    def passed(p, carry):
        @pl.when(p >= PIECES - AHEAD)
        def _():
            rows_left(p)

        forward(p, oth).wait_send()

        @pl.when(inner)
        def _():
            forward(p, own).wait_send()

        return carry

    lax.fori_loop(0, PIECES, passed, 0)

    def sent(u, carry):
        g, f, i = unit(u)

        x_copy(g, f, i).wait_send()

        @pl.when(g == 0)
        def _():
            for q in range(2):
                for j in range(2):
                    out0(j, q, f, i).wait_send()

        @pl.when(g > 0)
        def _():
            for q in range(2):
                out(g, q, f, i).wait_send()

        return carry

    lax.fori_loop(0, UNITS, sent, 0)

    def columns(f, yy, i, cc):
        first = f * 4 * wide + yy * 2 * wide + cc * wide + i * wrows
        return slice(first, first + wrows)

    for f in range(2):
        for i in range(2):
            for yy in range(2):
                for j in range(2):
                    remote(
                        csum.at[0, 0, 0, 0], obuf.at[yy, f, i, j], o_send0.at[0, 0, 0, 0],
                        o_recv0.at[j, yy, f, i], at(z, y, 1 - c, x),
                    ).wait_recv()
                for g in range(1, GROUPS):
                    remote(
                        csum.at[0, 0, 0, pl.ds(0, 2)], obuf.at[yy, f, i, pl.ds(2 * g, 2)], o_send.at[0, 0, 0, 0],
                        o_recv.at[g - 1, yy, f, i], at(z, y, 1 - c, x),
                    ).wait_recv()

    for slot in range(slots):
        rank = order_ref[slots + slot]
        for f in range(2):
            for i in range(2):
                for yy in range(2):
                    for cc in range(2):
                        o_ref[slot, :, columns(f, yy, i, cc)] = obuf[
                            yy, f, i, rank, :, cc * wrows : (cc + 1) * wrows
                        ]


def fused(queries, fresh_kv, pages, lengths, table, movers, w_out):
    slots, tokens, width = queries.shape
    wide = w_out.shape[0]
    kv_heads = fresh_kv.shape[2] // (2 * HEAD_SIZE)
    qrows = width // (kv_heads * HEAD_SIZE) * tokens
    rows = slots * tokens // GROUPS
    pool, page, maxp = pages.shape[0], pages.shape[1], table.shape[1]
    most = [-(-MOVER_POSITIONS // page)] * 2
    for i in range(slots - 2):
        most.append(min(maxp, (pool - 2 - i) // (slots - 2 - i)))
    rank_steps = tuple(-(-m // STEP_PAGES) for m in most)
    dma = pltpu.SemaphoreType.DMA
    smem, hbm = pl.BlockSpec(memory_space=pltpu.SMEM), pl.BlockSpec(memory_space=pl.ANY)
    b, f32 = jnp.bfloat16, jnp.float32
    done = pl.pallas_call(
        functools.partial(fused_kernel, rank_steps),
        out_shape=jax.ShapeDtypeStruct((slots, tokens, 8 * wide), b),
        in_specs=[hbm, hbm, hbm, smem, smem, smem, hbm],
        out_specs=pl.BlockSpec(memory_space=pltpu.VMEM),
        scratch_shapes=[
            pltpu.VMEM(queries.shape, b),
            pltpu.VMEM(fresh_kv.shape, b),
            pltpu.VMEM(pages.shape, b),
            pltpu.SMEM((2 * slots,), jnp.int32),
            pltpu.VMEM((kv_heads, qrows, HEAD_SIZE), b),
            pltpu.VMEM((max(rank_steps), kv_heads, qrows, STEP_PAGES * page), f32),
            pltpu.VMEM((kv_heads, qrows, HEAD_SIZE), f32),
            pltpu.VMEM((2, kv_heads, qrows, 1), f32),
            pltpu.VMEM((2, kv_heads, qrows, HEAD_SIZE), f32),
            pltpu.VMEM((2, kv_heads, qrows, HEAD_SIZE), f32),
            pltpu.VMEM((GROUPS, rows, width), b),
            pltpu.VMEM((GROUPS, 4, rows, width), b),
            pltpu.VMEM((2, 2, 2, wide // 2, width), b),
            pltpu.VMEM((GROUPS, 2, 2, 2 * rows, wide), b),
            pltpu.VMEM((GROUPS, 2, 2, 2 * rows, wide), b),
            pltpu.VMEM((GROUPS, 2, 2, 2 * rows, wide), f32),
            pltpu.VMEM((2, 2, 2, slots, tokens, wide), b),
            pltpu.VMEM((2, 2, 2, slots, tokens, wide), b),
            dma((2 + PAGE_COPIES,)), dma((2,)), dma((WPARTS,)), dma((WPARTS,)), dma((2, 2)), dma((2, 2)),
            dma((PIECES,)), dma((PIECES,)), dma((PIECES, 2)), dma((PIECES, 2)), dma((PIECES, 2)),
            dma((GROUPS, 2, 2)), dma((GROUPS, 2, 2)),
            dma((2, 2, 2, 2)), dma((GROUPS - 1, 2, 2, 2)), dma((2, 2, 2, 2)), dma((GROUPS - 1, 2, 2, 2)),
        ],
        compiler_params=pltpu.CompilerParams(
            collective_id=0, has_side_effects=True, vmem_limit_bytes=60 << 20
        ),
    )(queries, fresh_kv, pages, lengths, table, movers, w_out)
    return done.reshape(slots * tokens, 8 * wide)


def per_device(queries, fresh_kv, key_value_pages, cache_lengths, page_table, movers, w_out):
    slots, tokens, width = queries.shape
    to_next = movers[0, 0]
    to_prev = movers[0, 1]
    if lax.axis_size("tp") == 2 and lax.axis_size("req") == 16 and slots == 2 * GROUPS and key_value_pages.shape[0] % PAGE_COPIES == 0:
        return fused(queries, fresh_kv, key_value_pages, cache_lengths, page_table, movers, w_out)
    attended = attend(queries, fresh_kv, key_value_pages, cache_lengths, page_table)
    from_left = passed_along(attended[to_next], "req", 1)
    from_right = passed_along(attended[to_prev], "req", -1)
    slot_ids = jnp.arange(slots, dtype=jnp.int32)[:, None, None]
    placed = jnp.where(
        slot_ids == to_next, from_left[None], jnp.where(slot_ids == to_prev, from_right[None], attended)
    )
    flat = placed.reshape(slots * tokens, width)
    partial_sum = lax.dot_general(
        flat,
        lax.all_gather(w_out, "req", axis=0, tiled=True),
        (((1,), (1,)), ((), ())),
        preferred_element_type=jnp.float32,
    )
    return lax.psum_scatter(partial_sum, "tp", scatter_dimension=1, tiled=True).astype(jnp.bfloat16)


def solution(mesh):
    return jax.shard_map(
        per_device,
        mesh=mesh,
        in_specs=(
            P("req", None, "tp"),
            P("req", None, "tp"),
            P("req", None, "tp"),
            P("req"),
            P("req", None),
            P("req", None),
            P("req", "tp"),
        ),
        out_specs=P("req", "tp"),
        check_vma=False,
    )
```
